128 devices in a mesh: blk: 16 (over x, z), leaf: 8 (over y, core).
Axes of the slice: x: 4, y: 4, z: 4, core: 2. Of those that a mesh axis runs over, the one named last changes fastest.
Arguments:
- columns_in: bfloat16 [16, 8, 4096, 512], P('blk', 'leaf'), may hold values from -6 to 6
- leaf_basis: bfloat16 [16, 8, 32, 128, 128], P('blk', 'leaf'), may hold values from -0.5 to 0.5
- transfers: bfloat16 [16, 8, 8, 32, 128, 256], P('blk', None, 'leaf'), may hold values from -0.4375 to 0.4375
- row_basis: bfloat16 [16, 8, 32, 128, 128], P('blk', 'leaf'), may hold values from -0.15625 to 0.15625
- ranks: int32 [16, 9, 8, 32], P('blk', None, 'leaf'), may hold values from 64 to 128, as said below
- col_owner: int32 [8], replicated, may hold values from 0 to 7, each once
- row_owner: int32 [8], replicated, may hold values from 0 to 7, each once
Outputs:
- row_sums: bfloat16 [8, 4096, 512], P('leaf', 'blk')
The draws below stay inside these ranges and needn't reach their ends.
Inputs may be any that keep to these rules, and one draw needn't show every extreme that they name: ranks of every node of every level; the smallest and the largest value each occur. `col_owner`: each subtree number once. `row_owner`: each subtree number once.
All inputs are finite; a program needn't handle non-finite values.
Results may differ from the reference program's by a relative error of at most 0.019.
Values may be sent and summed in bfloat16 or wider, within the bound.
A program may use at most 128 MiB of HBM per device.

```python
import jax
import jax.numpy as jnp
from jax import lax

LEAF = 128
R = 128
LEVELS = 8
RHS = 512
MID = 4
OWNERS = 8
BLOCKS = 16
NODES_DEV = 32
SUB = 4096


def draw_ranks(key, part):
    shape = (BLOCKS, LEVELS + 1, OWNERS, NODES_DEV)
    base = jax.random.randint(key, shape, R // 2, R + 1).astype(jnp.int32)
    flat = base.reshape(-1)
    count = flat.shape[0]
    first = jax.random.randint(jax.random.fold_in(key, 11), (), 0, count)
    offset = jax.random.randint(jax.random.fold_in(key, 12), (), 1, count)
    second = (first + offset) % count
    flat = flat.at[first].set(R).at[second].set(R // 2)
    return flat.reshape(shape).astype(jnp.int32)


def block_levels(own_key, extent, split, smallest, largest):
    def one(dim, blocks):
        draws = jax.random.uniform(jax.random.fold_in(jax.random.fold_in(own_key, 6), dim), (blocks,), jnp.float32, smallest / len(split), largest / len(split))
        return jnp.repeat(jnp.exp(draws), extent[dim] // blocks).reshape((-1,) + (1,) * (len(extent) - dim - 1))

    level = one(*split[0])
    for cut in split[1:]:
        level = level * one(*cut)
    return level


def noise(key, extent, width, most, pieces=(), held_as=jnp.bfloat16):
    drawn = width * jax.random.normal(key, extent, jnp.float32)
    if pieces:
        drawn = drawn * block_levels(key, extent, pieces, -0.22, 0.18)
    return jnp.clip(drawn, -most, most).astype(held_as)


def setup_inputs(seed: int = 0) -> dict:
    seeds = jax.random.split(jax.random.key(seed), 8)
    return {
        "columns_in": noise(seeds[0], (BLOCKS, OWNERS, SUB, RHS), 1.0, 6.0, ((0, 16), (1, 8))),
        "leaf_basis": noise(seeds[1], (BLOCKS, OWNERS, NODES_DEV, LEAF, R), LEAF ** -0.5, 0.5, ((0, 16), (1, 8))),
        "transfers": noise(seeds[2], (BLOCKS, LEVELS, OWNERS, NODES_DEV, R, 2 * R), (3 * R // 2) ** -0.5, 0.4375, ((0, 16), (2, 8))),
        "row_basis": noise(seeds[3], (BLOCKS, OWNERS, NODES_DEV, LEAF, R), (3 * R * BLOCKS // 4) ** -0.5, 0.15625, ((0, 16), (1, 8))),
        "ranks": draw_ranks(jax.random.fold_in(seeds[7], 71), 0),
        "col_owner": jax.random.permutation(seeds[5], OWNERS).astype(jnp.int32),
        "row_owner": jax.random.permutation(seeds[6], OWNERS).astype(jnp.int32),
    }


def apply_ranks(coeffs, live):
    row_ids = jnp.arange(coeffs.shape[-2], dtype=jnp.int32)
    keep = (row_ids[:, None] < live[..., None, None]).astype(jnp.float32)
    return coeffs * keep


def one_block(inputs, leaf_basis, transfers, row_basis, ranks, col_owner, row_owner):
    owners = OWNERS
    nodes_local = NODES_DEV
    values = inputs.reshape(owners, nodes_local, LEAF, RHS).astype(jnp.float32)
    current = jnp.einsum('onlr,onlh->onrh', leaf_basis.astype(jnp.float32), values)
    coeffs = apply_ranks(current, ranks[0]).astype(jnp.bfloat16)
    for level_index in range(1, MID + 1):
        half_j = 2 ** (LEVELS - level_index) // owners
        half_i = 2 ** (level_index - 1)
        previous = coeffs.astype(jnp.float32).reshape(owners, half_j, 2, half_i, R, RHS)
        mixing = transfers[level_index - 1].astype(jnp.float32).reshape(owners, half_j, half_i, 2, R, 2, R)
        live = ranks[level_index]
        if level_index < MID:
            current = jnp.einsum('ojibrtq,ojtiqh->ojibrh', mixing, previous)
        else:
            current = jnp.einsum('ojibrtq,ojtiqh->oibjrh', mixing, previous)
            live = live.reshape(owners, half_j, half_i, 2).transpose(0, 2, 3, 1)
        coeffs = apply_ranks(current.reshape(owners, nodes_local, R, RHS), live.reshape(owners, nodes_local)).astype(jnp.bfloat16)
    sub_i = 2 ** MID // owners
    part_j = 2 ** (LEVELS - MID) // owners
    grouped = coeffs.reshape(owners, owners, sub_i, part_j, R, RHS)
    outgoing = jnp.take(grouped, row_owner.astype(jnp.int32), axis=1)
    incoming = jnp.transpose(outgoing, (1, 2, 0, 3, 4, 5))
    inverse = jnp.argsort(col_owner).astype(jnp.int32)
    coeffs = jnp.take(incoming, inverse, axis=2).reshape(owners, nodes_local, R, RHS)
    for level_index in range(MID + 1, LEVELS + 1):
        half_i = 2 ** (level_index - 1) // owners
        half_j = 2 ** (LEVELS - level_index)
        previous = coeffs.astype(jnp.float32).reshape(owners, half_i, half_j, 2, R, RHS)
        mixing = transfers[level_index - 1].astype(jnp.float32).reshape(owners, half_i, 2, half_j, R, 2, R)
        current = jnp.einsum('oibjrtq,oijtqh->oibjrh', mixing, previous)
        coeffs = apply_ranks(current.reshape(owners, nodes_local, R, RHS), ranks[level_index]).astype(jnp.bfloat16)
    result = jnp.einsum('onlr,onrh->onlh', row_basis.astype(jnp.float32), coeffs.astype(jnp.float32))
    return result.reshape(owners, SUB, RHS)


def reference(columns_in, leaf_basis, transfers, row_basis, ranks, col_owner, row_owner):
    def add_block(total, items):
        inputs, leaves, mixers, rows_basis, rank_table = items
        return total + one_block(inputs, leaves, mixers, rows_basis, rank_table, col_owner, row_owner), None

    start_total = jnp.zeros((OWNERS, SUB, RHS), jnp.float32)
    total, unused = lax.scan(add_block, start_total, (columns_in, leaf_basis, transfers, row_basis, ranks))
    return total.astype(jnp.bfloat16)
```

```python
import functools

import jax
import jax.numpy as jnp
from jax import lax
from jax.experimental import pallas as pl
from jax.experimental.pallas import tpu as pltpu
from jax.sharding import PartitionSpec as P

MESH = pl.DeviceIdType.MESH
SIDE = 4
PEERS = (4, 3, 5, 2, 6, 1, 7)
QUARTERS = (2, 1, 3, 0)


def dot(a, b):
    return jnp.dot(a, b, preferred_element_type=jnp.float32)


def kernel(
    chunks, width, rank,
    x_hbm, leaf_hbm, mix_hbm, row_hbm, ranks, col_owner, row_owner,
    out,
    xv, leaf, t1, t2, t3, t4, t5, t6, t7, t8, row,
    ca, cb, send, recv, c5, c6, c7, c8,
    xs, zs, xr, zr, xs2, zs2, xr2, zr2,
    in_sem, x_sem,
    a_send, a_recv, xs_sem, xr_sem, zs_sem, zr_sem, xs2_sem, xr2_sem, zs2_sem, zr2_sem,
):
    mixes = (t1, t2, t3, t4, t5, t6, t7, t8)
    me = lax.axis_index("leaf")
    blk = lax.axis_index("blk")
    bx, bz = lax.div(blk, SIDE), lax.rem(blk, SIDE)

    def leaf_peer(d):
        return {"blk": blk, "leaf": lax.rem(me + d, 8)}

    def x_peer(d):
        return {"blk": lax.rem(bx + d, SIDE) * SIDE + bz, "leaf": me}

    def z_peer(d):
        return {"blk": bx * SIDE + lax.rem(bz + d, SIDE), "leaf": me}

    def x_in(c):
        return pltpu.make_async_copy(
            x_hbm.at[:, :, pl.ds(pl.multiple_of(c * width, width), width)],
            xv.at[c], x_sem.at[c])

    def weight_in(i):
        if i == 0:
            return pltpu.make_async_copy(leaf_hbm, leaf, in_sem.at[0])
        if i == 9:
            return pltpu.make_async_copy(row_hbm, row, in_sem.at[9])
        return pltpu.make_async_copy(mix_hbm.at[i - 1], mixes[i - 1], in_sem.at[i])

    weight_in(0).start()
    x_in(0).start()
    for i in range(1, 5):
        weight_in(i).start()
    for c in range(1, chunks):
        x_in(c).start()
    for i in range(5, 10):
        weight_in(i).start()

    barrier = pltpu.get_barrier_semaphore()
    for d in range(1, 8):
        pl.semaphore_signal(barrier, inc=1, device_id=leaf_peer(d), device_id_type=MESH)
    for d in range(1, SIDE):
        pl.semaphore_signal(barrier, inc=1, device_id=x_peer(d), device_id_type=MESH)
        pl.semaphore_signal(barrier, inc=1, device_id=z_peer(d), device_id_type=MESH)

    row_ids = lax.broadcasted_iota(jnp.int32, (rank, width), 0)

    def keep(value, live):
        return jnp.where(row_ids < live, value, 0.0).astype(jnp.bfloat16)

    def mix(lhs, top, bottom):
        return dot(lhs, jnp.concatenate([top, bottom], axis=0))

    def pair(ref, p):
        return ref[pl.ds(2 * p, 2)].reshape(2 * rank, 2 * rank)

    def leaf_level(c):
        @pl.loop(0, 8)
        def _(g):
            for u in range(4):
                n = 4 * g + u
                value = lax.dot_general(
                    leaf[n], xv[c, n], (((0,), (0,)), ((), ())),
                    preferred_element_type=jnp.float32)
                ca[n] = keep(value, ranks[0, n])

    def column_level(level, source, target):
        half_i = 2 ** (level - 1)

        @pl.loop(0, 4)
        def _(g):
            for u in range(4):
                p = 4 * g + u
                a = (p // half_i) * (2 * half_i) + p % half_i
                value = mix(pair(mixes[level - 1], p), source[a], source[a + half_i])
                target[2 * p] = keep(value[:rank], ranks[level, 2 * p])
                target[2 * p + 1] = keep(value[rank:], ranks[level, 2 * p + 1])

    def a2a(c, d):
        return pltpu.make_async_remote_copy(
            src_ref=send.at[c, d], dst_ref=recv.at[c, d - 1],
            send_sem=a_send.at[c, d - 1], recv_sem=a_recv.at[c, d - 1],
            device_id=leaf_peer(d), device_id_type=MESH)

    def switch_level(c, source):
        waiting = None
        for d in PEERS + (0,):
            s = row_owner[lax.rem(me + d, 8)]
            for j in range(2):
                node = j * 8 + s
                value = mix(pair(t4, node), source[2 * j * 8 + s], source[(2 * j + 1) * 8 + s])
                send[c, d, j] = keep(value[:rank], ranks[4, 2 * node])
                send[c, d, 2 + j] = keep(value[rank:], ranks[4, 2 * node + 1])
            if waiting is not None:
                a2a(c, waiting).start()
            waiting = d

    def phase_a(c):
        x_in(c).wait()

        @pl.when(c == 0)
        def _():
            weight_in(0).wait()

        leaf_level(c)
        for level, source, target in ((1, ca, cb), (2, cb, ca), (3, ca, cb)):
            @pl.when(c == 0)
            def _():
                weight_in(level).wait()

            column_level(level, source, target)

        @pl.when(c == 0)
        def _():
            weight_in(4).wait()
            pl.semaphore_wait(barrier, 7 + 2 * (SIDE - 1))

        switch_level(c, cb)

    def x_first(c, d):
        return pltpu.make_async_remote_copy(
            src_ref=xs.at[c, d], dst_ref=xr.at[c, d - 1],
            send_sem=xs_sem.at[c, d - 1], recv_sem=xr_sem.at[c, d - 1],
            device_id=x_peer(d), device_id_type=MESH)

    def z_first(c, d):
        return pltpu.make_async_remote_copy(
            src_ref=zs.at[c, d], dst_ref=zr.at[c, d - 1],
            send_sem=zs_sem.at[c, d - 1], recv_sem=zr_sem.at[c, d - 1],
            device_id=z_peer(d), device_id_type=MESH)

    def z_second(c, d):
        return pltpu.make_async_remote_copy(
            src_ref=zs2.at[c, d], dst_ref=zr2.at[c, d - 1],
            send_sem=zs2_sem.at[c, d - 1], recv_sem=zr2_sem.at[c, d - 1],
            device_id=z_peer(d), device_id_type=MESH)

    def x_second(c, d):
        return pltpu.make_async_remote_copy(
            src_ref=xs2.at[c, d], dst_ref=xr2.at[c, d - 1],
            send_sem=xs2_sem.at[c, d - 1], recv_sem=xr2_sem.at[c, d - 1],
            device_id=x_peer(d), device_id_type=MESH)

    def arrive(c, d):
        owner = lax.rem(me + 8 - d, 8)
        j = col_owner[owner]
        for i in range(2):
            lhs = jnp.concatenate([t5[2 * i * 8 + j], t5[(2 * i + 1) * 8 + j]], axis=0)
            if d == 0:
                nodes = send[c, 0, pl.ds(2 * i, 2)]
            else:
                nodes = recv[c, d - 1, pl.ds(2 * i, 2)]
            value = dot(lhs, nodes.reshape(2 * rank, width))
            for e in range(2):
                c5[2 * i + e, d] = keep(
                    value[e * rank:(e + 1) * rank], ranks[5, (2 * i + e) * 8 + j])

    def quarter(c, dq, places):
        q = lax.rem(bx + dq, SIDE)
        for j in range(4):
            lhs = jnp.concatenate([t6[2 * q * 4 + j], t6[(2 * q + 1) * 4 + j]], axis=0)
            value = mix(lhs, c5[q, places[2 * j]], c5[q, places[2 * j + 1]])
            for e in range(2):
                c6[e * 4 + j] = keep(
                    value[e * rank:(e + 1) * rank], ranks[6, (2 * q + e) * 4 + j])
        for i in range(2):
            for j in range(2):
                base = (2 * q + i) * 4 + j
                lhs = jnp.concatenate([t7[base], t7[base + 2]], axis=0)
                value = mix(lhs, c6[i * 4 + 2 * j], c6[i * 4 + 2 * j + 1])
                for e in range(2):
                    c7[(i * 2 + e) * 2 + j] = keep(
                        value[e * rank:(e + 1) * rank], ranks[7, base + 2 * e])
        for i in range(4):
            node = 4 * q + i
            value = mix(pair(t8, node), c7[2 * i], c7[2 * i + 1])
            for e in range(2):
                c8[2 * i + e] = keep(
                    value[e * rank:(e + 1) * rank], ranks[8, 2 * node + e])
        for m in range(4):
            xs[c, dq, m] = dot(row[8 * q + 2 * m], c8[2 * m]).astype(jnp.bfloat16)
        for r in range(SIDE):
            m = lax.rem(bz + r, SIDE)
            zs[c, r, dq] = dot(row[8 * q + 2 * m + 1], c8[2 * m + 1]).astype(jnp.bfloat16)

    def phase_b(c):
        @pl.when(c == 0)
        def _():
            for i in range(5, 10):
                weight_in(i).wait()

        arrive(c, 0)
        for d in (7, 1, 6, 2, 5, 3, 4):
            a2a(c, d).wait_recv()
            arrive(c, d)
        places = []
        for wanted in range(8):
            found = jnp.int32(0)
            for o in range(8):
                found = found + jnp.where(col_owner[o] == wanted, o, 0)
            places.append(lax.rem(me + 32 - found, 8))
        for index, dq in enumerate(QUARTERS):
            quarter(c, dq, places)
            if index:
                x_first(c, QUARTERS[index - 1]).start()
        for d in (2, 1, 3):
            z_first(c, d).start()

    def wide(value):
        return value.astype(jnp.float32)

    def first_sum(c):
        for d in (2, 1, 3):
            x_first(c, d).wait_recv()
        for r in (2, 1, 3, 0):
            m = lax.rem(bz + r, SIDE)
            total = wide(xs[c, 0, m])
            for d in range(SIDE - 1):
                total = total + wide(xr[c, d, m])
            zs2[c, r] = total.astype(jnp.bfloat16)
        for d in (2, 1, 3):
            z_second(c, d).start()
        for d in (2, 1, 3):
            z_first(c, d).wait_recv()
        for r in (2, 1, 3, 0):
            total = wide(zs[c, 0, r])
            for d in range(SIDE - 1):
                total = total + wide(zr[c, d, r])
            xs2[c, r] = total.astype(jnp.bfloat16)
        for d in (2, 1, 3):
            x_second(c, d).start()

    def last_sum(c):
        columns = pl.ds(pl.multiple_of(c * width, width), width)
        for d in (1, 3, 2):
            z_second(c, d).wait_recv()
        total = wide(zs2[c, 0])
        for d in range(SIDE - 1):
            total = total + wide(zr2[c, d])
        out[pl.ds(0, rank), columns] = total.astype(jnp.bfloat16)
        for d in (1, 3, 2):
            x_second(c, d).wait_recv()
        total = wide(xs2[c, 0])
        for d in range(SIDE - 1):
            total = total + wide(xr2[c, d])
        out[pl.ds(rank, rank), columns] = total.astype(jnp.bfloat16)

    @pl.loop(0, chunks)
    def _(c):
        phase_a(c)

    @pl.loop(0, chunks)
    def _(c):
        @pl.when(c >= 1)
        def _():
            first_sum(c - 1)

        phase_b(c)

        @pl.when(c >= 1)
        def _():
            last_sum(c - 1)

    first_sum(chunks - 1)
    last_sum(chunks - 1)

    @pl.loop(0, chunks)
    def _(c):
        for d in range(1, 8):
            a2a(c, d).wait_send()
        for d in range(1, SIDE):
            x_first(c, d).wait_send()
            z_first(c, d).wait_send()
            x_second(c, d).wait_send()
            z_second(c, d).wait_send()


def local(columns_in, leaf_basis, transfers, row_basis, ranks, col_owner, row_owner):
    nodes, leaf_size, rank = leaf_basis.shape[2:]
    sides = columns_in.shape[3]
    levels = transfers.shape[1]
    width = 128
    chunks = sides // width
    bf = jnp.bfloat16
    dma = pltpu.SemaphoreType.DMA
    hbm = pl.BlockSpec(memory_space=pltpu.HBM)
    smem = pl.BlockSpec(memory_space=pltpu.SMEM)
    tile = (rank, width)
    scratch = [pltpu.VMEM((chunks, nodes, leaf_size, width), bf), pltpu.VMEM((nodes, leaf_size, rank), bf)]
    scratch += [pltpu.VMEM((nodes, rank, 2 * rank), bf)] * levels
    scratch += [pltpu.VMEM((nodes, leaf_size, rank), bf)]
    scratch += [pltpu.VMEM((nodes,) + tile, bf)] * 2
    scratch += [pltpu.VMEM((chunks, 8, 4) + tile, bf), pltpu.VMEM((chunks, 7, 4) + tile, bf)]
    scratch += [pltpu.VMEM((4, 8) + tile, bf)] + [pltpu.VMEM((8,) + tile, bf)] * 3
    scratch += [pltpu.VMEM((chunks, 4, 4) + tile, bf)] * 2
    scratch += [pltpu.VMEM((chunks, 3, 4) + tile, bf)] * 2
    scratch += [pltpu.VMEM((chunks, 4) + tile, bf)] * 2
    scratch += [pltpu.VMEM((chunks, 3) + tile, bf)] * 2
    scratch += [dma((10,)), dma((chunks,)), dma((chunks, 7)), dma((chunks, 7))]
    scratch += [dma((chunks, 3))] * 8
    share = nodes * leaf_size // lax.axis_size("blk")
    result = pl.pallas_call(
        functools.partial(kernel, chunks, width, rank),
        out_shape=jax.ShapeDtypeStruct((share, sides), bf),
        in_specs=[hbm] * 4 + [smem] * 3,
        out_specs=pl.BlockSpec(memory_space=pltpu.VMEM),
        scratch_shapes=scratch,
        compiler_params=pltpu.CompilerParams(
            collective_id=0, has_side_effects=True, vmem_limit_bytes=60 * 1024 * 1024),
        name="block_row",
    )(
        columns_in.reshape(nodes, leaf_size, sides),
        leaf_basis[0, 0],
        transfers[0, :, 0],
        row_basis[0, 0],
        ranks[0, :, 0],
        col_owner,
        row_owner,
    )
    return result.reshape(1, share, sides)


def solution(mesh):
    return jax.shard_map(
        local,
        mesh=mesh,
        in_specs=(
            P("blk", "leaf", None, None),
            P("blk", "leaf", None, None, None),
            P("blk", None, "leaf", None, None, None),
            P("blk", "leaf", None, None, None),
            P("blk", None, "leaf", None),
            P(),
            P(),
        ),
        out_specs=P("leaf", "blk", None),
        check_vma=False,
    )
```

```python
import functools

import jax
import jax.numpy as jnp
from jax import lax
from jax.experimental import pallas as pl
from jax.experimental.pallas import tpu as pltpu
from jax.sharding import PartitionSpec as P

MESH = pl.DeviceIdType.MESH
SIDE = 4
PEERS = (4, 3, 5, 2, 6, 1, 7)
QUARTERS = (2, 1, 3, 0)


def dot(a, b):
    return jnp.dot(a, b, preferred_element_type=jnp.float32)


def kernel(
    chunks, width, wide_width, rank,
    x_hbm, leaf_hbm, mix_hbm, row_hbm, ranks, col_owner, row_owner,
    out,
    xv, leaf, t1, t2, t3, t4, t5, t6, t7, t8, row,
    ca, cb, send, recv, c5, c6, c7, c8,
    xs, zs, xr, zr, xs2, zs2, xr2, zr2,
    in_sem, x_sem,
    a_send, a_recv, xs_sem, xr_sem, zs_sem, zr_sem, xs2_sem, xr2_sem, zs2_sem, zr2_sem,
):
    mixes = (t1, t2, t3, t4, t5, t6, t7, t8)
    me = lax.axis_index("leaf")
    blk = lax.axis_index("blk")
    bx, bz = lax.div(blk, SIDE), lax.rem(blk, SIDE)

    def leaf_peer(d):
        return {"blk": blk, "leaf": lax.rem(me + d, 8)}

    def x_peer(d):
        return {"blk": lax.rem(bx + d, SIDE) * SIDE + bz, "leaf": me}

    def z_peer(d):
        return {"blk": bx * SIDE + lax.rem(bz + d, SIDE), "leaf": me}

    halves = wide_width // width

    def x_in(w):
        return pltpu.make_async_copy(
            x_hbm.at[:, :, pl.ds(pl.multiple_of(w * wide_width, wide_width), wide_width)],
            xv.at[w], x_sem.at[w])

    def weight_in(i):
        if i == 0:
            return pltpu.make_async_copy(leaf_hbm, leaf, in_sem.at[0])
        if i == 9:
            return pltpu.make_async_copy(row_hbm, row, in_sem.at[9])
        return pltpu.make_async_copy(mix_hbm.at[i - 1], mixes[i - 1], in_sem.at[i])

    weight_in(0).start()
    x_in(0).start()
    for i in range(1, 5):
        weight_in(i).start()
    for w in range(1, chunks // halves):
        x_in(w).start()
    for i in range(5, 10):
        weight_in(i).start()

    barrier = pltpu.get_barrier_semaphore()
    for d in range(1, 8):
        pl.semaphore_signal(barrier, inc=1, device_id=leaf_peer(d), device_id_type=MESH)
    for d in range(1, SIDE):
        pl.semaphore_signal(barrier, inc=1, device_id=x_peer(d), device_id_type=MESH)
        pl.semaphore_signal(barrier, inc=1, device_id=z_peer(d), device_id_type=MESH)

    places = []
    for wanted in range(8):
        found = jnp.int32(0)
        for o in range(8):
            found = found + jnp.where(col_owner[o] == wanted, o, 0)
        places.append(lax.rem(me + 32 - found, 8))

    def keep(value, live):
        row_ids = lax.broadcasted_iota(jnp.int32, value.shape, 0)
        return jnp.where(row_ids < live, value, 0.0).astype(jnp.bfloat16)

    def mix(lhs, top, bottom):
        return dot(lhs, jnp.concatenate([top, bottom], axis=0))

    def pair(ref, p):
        return ref[pl.ds(2 * p, 2)].reshape(2 * rank, 2 * rank)

    def leaf_level(w):
        @pl.loop(0, 4)
        def _(g):
            for u in range(8):
                n = 8 * g + u
                value = lax.dot_general(
                    leaf[n], xv[w, n], (((0,), (0,)), ((), ())),
                    preferred_element_type=jnp.float32)
                ca[n] = keep(value, ranks[0, n])

    def column_level(level, source, target):
        half_i = 2 ** (level - 1)

        @pl.loop(0, 2)
        def _(g):
            for u in range(8):
                p = 8 * g + u
                a = 16 * g + (u // half_i) * (2 * half_i) + u % half_i
                value = mix(pair(mixes[level - 1], p), source[a], source[a + half_i])
                target[2 * p] = keep(value[:rank], ranks[level, 2 * p])
                target[2 * p + 1] = keep(value[rank:], ranks[level, 2 * p + 1])

    def a2a(c, d):
        return pltpu.make_async_remote_copy(
            src_ref=send.at[c, d], dst_ref=recv.at[c, d - 1],
            send_sem=a_send.at[c, d - 1], recv_sem=a_recv.at[c, d - 1],
            device_id=leaf_peer(d), device_id_type=MESH)

    def switch_level(w, source):
        waiting = None
        for d in PEERS + (0,):
            s = row_owner[lax.rem(me + d, 8)]
            for j in range(2):
                node = j * 8 + s
                value = mix(pair(t4, node), source[2 * j * 8 + s], source[(2 * j + 1) * 8 + s])
                for e in range(2):
                    kept = keep(value[e * rank:(e + 1) * rank], ranks[4, 2 * node + e])
                    for h in range(halves):
                        send[w * halves + h, d, 2 * e + j] = kept[:, h * width:(h + 1) * width]
            if waiting is not None:
                a2a(w * halves, waiting).start()
            waiting = d
        for h in range(1, halves):
            for d in PEERS:
                a2a(w * halves + h, d).start()

    def phase_a(w):
        x_in(w).wait()

        @pl.when(w == 0)
        def _():
            weight_in(0).wait()

        leaf_level(w)
        for level, source, target in ((1, ca, cb), (2, cb, ca), (3, ca, cb)):
            @pl.when(w == 0)
            def _():
                weight_in(level).wait()

            column_level(level, source, target)

        @pl.when(w == 0)
        def _():
            weight_in(4).wait()
            pl.semaphore_wait(barrier, 7 + 2 * (SIDE - 1))

        switch_level(w, cb)

    def x_first(c, d):
        return pltpu.make_async_remote_copy(
            src_ref=xs.at[c, d], dst_ref=xr.at[c, d - 1],
            send_sem=xs_sem.at[c, d - 1], recv_sem=xr_sem.at[c, d - 1],
            device_id=x_peer(d), device_id_type=MESH)

    def z_first(c, d, half):
        return pltpu.make_async_remote_copy(
            src_ref=zs.at[c, d, pl.ds(2 * half, 2)], dst_ref=zr.at[c, d - 1, pl.ds(2 * half, 2)],
            send_sem=zs_sem.at[c, d - 1, half], recv_sem=zr_sem.at[c, d - 1, half],
            device_id=z_peer(d), device_id_type=MESH)

    def z_second(c, d):
        return pltpu.make_async_remote_copy(
            src_ref=zs2.at[c, d], dst_ref=zr2.at[c, d - 1],
            send_sem=zs2_sem.at[c, d - 1], recv_sem=zr2_sem.at[c, d - 1],
            device_id=z_peer(d), device_id_type=MESH)

    def x_second(c, d):
        return pltpu.make_async_remote_copy(
            src_ref=xs2.at[c, d], dst_ref=xr2.at[c, d - 1],
            send_sem=xs2_sem.at[c, d - 1], recv_sem=xr2_sem.at[c, d - 1],
            device_id=x_peer(d), device_id_type=MESH)

    def arrive(c, d):
        owner = lax.rem(me + 8 - d, 8)
        j = col_owner[owner]
        for i in range(2):
            lhs = jnp.concatenate([t5[2 * i * 8 + j], t5[(2 * i + 1) * 8 + j]], axis=0)
            if d == 0:
                nodes = send[c, 0, pl.ds(2 * i, 2)]
            else:
                nodes = recv[c, d - 1, pl.ds(2 * i, 2)]
            value = dot(lhs, nodes.reshape(2 * rank, width))
            for e in range(2):
                c5[2 * i + e, d] = keep(
                    value[e * rank:(e + 1) * rank], ranks[5, (2 * i + e) * 8 + j])

    def quarters(c, half):
        turns = tuple((k, dq, lax.rem(bx + dq, SIDE)) for k, dq in enumerate(QUARTERS[2 * half:2 * half + 2]))
        for k, dq, q in turns:
            for j in range(4):
                lhs = jnp.concatenate([t6[2 * q * 4 + j], t6[(2 * q + 1) * 4 + j]], axis=0)
                value = mix(lhs, c5[q, places[2 * j]], c5[q, places[2 * j + 1]])
                for e in range(2):
                    c6[k, e * 4 + j] = keep(
                        value[e * rank:(e + 1) * rank], ranks[6, (2 * q + e) * 4 + j])
        for k, dq, q in turns:
            for i in range(2):
                for j in range(2):
                    base = (2 * q + i) * 4 + j
                    lhs = jnp.concatenate([t7[base], t7[base + 2]], axis=0)
                    value = mix(lhs, c6[k, i * 4 + 2 * j], c6[k, i * 4 + 2 * j + 1])
                    for e in range(2):
                        c7[k, (i * 2 + e) * 2 + j] = keep(
                            value[e * rank:(e + 1) * rank], ranks[7, base + 2 * e])
        for k, dq, q in turns:
            for i in range(4):
                node = 4 * q + i
                value = mix(pair(t8, node), c7[k, 2 * i], c7[k, 2 * i + 1])
                for e in range(2):
                    c8[k, 2 * i + e] = keep(
                        value[e * rank:(e + 1) * rank], ranks[8, 2 * node + e])
        for k, dq, q in turns:
            for m in range(4):
                xs[c, dq, m] = dot(row[8 * q + 2 * m], c8[k, 2 * m]).astype(jnp.bfloat16)
        for k, dq, q in turns:
            for r in range(SIDE):
                m = lax.rem(bz + r, SIDE)
                zs[c, r, 2 * half + k] = dot(
                    row[8 * q + 2 * m + 1], c8[k, 2 * m + 1]).astype(jnp.bfloat16)
        for k, dq, q in turns:
            if dq:
                x_first(c, dq).start()
        for d in (2, 1, 3):
            z_first(c, d, half).start()

    def phase_b(c):
        @pl.when(c == 0)
        def _():
            for i in range(5, 10):
                weight_in(i).wait()

        arrive(c, 0)
        for d in (7, 1, 6, 2, 5, 3, 4):
            a2a(c, d).wait_recv()
            arrive(c, d)
        quarters(c, 0)
        quarters(c, 1)

    def wide(value):
        return value.astype(jnp.float32)

    def first_sum(c):
        for d in (2, 1, 3):
            x_first(c, d).wait_recv()
        for r in (2, 1, 3, 0):
            m = lax.rem(bz + r, SIDE)
            total = wide(xs[c, 0, m])
            for d in range(SIDE - 1):
                total = total + wide(xr[c, d, m])
            zs2[c, r] = total.astype(jnp.bfloat16)
        for d in (2, 1, 3):
            z_second(c, d).start()
        for d in (2, 1, 3):
            for half in range(2):
                z_first(c, d, half).wait_recv()
        for r in (2, 1, 3, 0):
            slot = QUARTERS.index(r)
            total = wide(zs[c, 0, slot])
            for d in range(SIDE - 1):
                total = total + wide(zr[c, d, slot])
            xs2[c, r] = total.astype(jnp.bfloat16)
        for d in (2, 1, 3):
            x_second(c, d).start()

    def last_sum(c):
        columns = pl.ds(pl.multiple_of(c * width, width), width)
        for d in (1, 3, 2):
            z_second(c, d).wait_recv()
        total = wide(zs2[c, 0])
        for d in range(SIDE - 1):
            total = total + wide(zr2[c, d])
        out[pl.ds(0, rank), columns] = total.astype(jnp.bfloat16)
        for d in (1, 3, 2):
            x_second(c, d).wait_recv()
        total = wide(xs2[c, 0])
        for d in range(SIDE - 1):
            total = total + wide(xr2[c, d])
        out[pl.ds(rank, rank), columns] = total.astype(jnp.bfloat16)

    @pl.loop(0, chunks // halves)
    def _(w):
        phase_a(w)

    @pl.loop(0, chunks)
    def _(c):
        @pl.when(c >= 1)
        def _():
            first_sum(c - 1)

        phase_b(c)

        @pl.when(c >= 1)
        def _():
            last_sum(c - 1)

    first_sum(chunks - 1)
    last_sum(chunks - 1)

    @pl.loop(0, chunks)
    def _(c):
        for d in range(1, 8):
            a2a(c, d).wait_send()
        for d in range(1, SIDE):
            x_first(c, d).wait_send()
            for half in range(2):
                z_first(c, d, half).wait_send()
            x_second(c, d).wait_send()
            z_second(c, d).wait_send()


def local(columns_in, leaf_basis, transfers, row_basis, ranks, col_owner, row_owner):
    nodes, leaf_size, rank = leaf_basis.shape[2:]
    sides = columns_in.shape[3]
    levels = transfers.shape[1]
    width = 128
    chunks = sides // width
    wide_width = 2 * width
    bf = jnp.bfloat16
    dma = pltpu.SemaphoreType.DMA
    hbm = pl.BlockSpec(memory_space=pltpu.HBM)
    smem = pl.BlockSpec(memory_space=pltpu.SMEM)
    tile = (rank, width)
    scratch = [pltpu.VMEM((sides // wide_width, nodes, leaf_size, wide_width), bf), pltpu.VMEM((nodes, leaf_size, rank), bf)]
    scratch += [pltpu.VMEM((nodes, rank, 2 * rank), bf)] * levels
    scratch += [pltpu.VMEM((nodes, leaf_size, rank), bf)]
    scratch += [pltpu.VMEM((nodes, rank, wide_width), bf)] * 2
    scratch += [pltpu.VMEM((chunks, 8, 4) + tile, bf), pltpu.VMEM((chunks, 7, 4) + tile, bf)]
    scratch += [pltpu.VMEM((4, 8) + tile, bf)] + [pltpu.VMEM((2, 8) + tile, bf)] * 3
    scratch += [pltpu.VMEM((chunks, 4, 4) + tile, bf)] * 2
    scratch += [pltpu.VMEM((chunks, 3, 4) + tile, bf)] * 2
    scratch += [pltpu.VMEM((chunks, 4) + tile, bf)] * 2
    scratch += [pltpu.VMEM((chunks, 3) + tile, bf)] * 2
    scratch += [dma((10,)), dma((sides // wide_width,)), dma((chunks, 7)), dma((chunks, 7))]
    scratch += [dma((chunks, 3))] * 2 + [dma((chunks, 3, 2))] * 2 + [dma((chunks, 3))] * 4
    share = nodes * leaf_size // lax.axis_size("blk")
    result = pl.pallas_call(
        functools.partial(kernel, chunks, width, wide_width, rank),
        out_shape=jax.ShapeDtypeStruct((share, sides), bf),
        in_specs=[hbm] * 4 + [smem] * 3,
        out_specs=pl.BlockSpec(memory_space=pltpu.VMEM),
        scratch_shapes=scratch,
        compiler_params=pltpu.CompilerParams(
            collective_id=0, has_side_effects=True, vmem_limit_bytes=60 * 1024 * 1024),
        name="block_row",
    )(
        columns_in.reshape(nodes, leaf_size, sides),
        leaf_basis[0, 0],
        transfers[0, :, 0],
        row_basis[0, 0],
        ranks[0, :, 0],
        col_owner,
        row_owner,
    )
    return result.reshape(1, share, sides)


def solution(mesh):
    return jax.shard_map(
        local,
        mesh=mesh,
        in_specs=(
            P("blk", "leaf", None, None),
            P("blk", "leaf", None, None, None),
            P("blk", None, "leaf", None, None, None),
            P("blk", "leaf", None, None, None),
            P("blk", None, "leaf", None),
            P(),
            P(),
        ),
        out_specs=P("leaf", "blk", None),
        check_vma=False,
    )
```

```python
import functools

import jax
import jax.numpy as jnp
from jax import lax
from jax.experimental import pallas as pl
from jax.experimental.pallas import tpu as pltpu
from jax.sharding import PartitionSpec as P

MESH = pl.DeviceIdType.MESH
SIDE = 4
PEERS = (4, 3, 5, 2, 6, 1, 7)


def dot(a, b):
    return jnp.dot(a, b, preferred_element_type=jnp.float32)


def kernel(
    chunks, width, wide_width, rank,
    x_hbm, leaf_hbm, mix_hbm, row_hbm, ranks, col_owner, row_owner,
    out,
    xv, leaf, t1, t2, t3, t4, t5, t6, t7, t8, row,
    ca, cb, send, recv, c5, c6, c7, c8,
    xs, zs, xr, zr, xs2, zs2, xr2, zr2,
    in_sem, x_sem,
    a_send, a_recv, xs_sem, xr_sem, zs_sem, zr_sem, xs2_sem, xr2_sem, zs2_sem, zr2_sem,
):
    mixes = (t1, t2, t3, t4, t5, t6, t7, t8)
    me = lax.axis_index("leaf")
    blk = lax.axis_index("blk")
    bx, bz = lax.div(blk, SIDE), lax.rem(blk, SIDE)

    odd = lax.rem(bx, 2)
    turns = ((2, 3 - 2 * odd), (1 + 2 * odd, 0))
    x_pair = lax.div(bx, 2)
    parts = (1 - x_pair, x_pair)

    def leaf_peer(d):
        return {"blk": blk, "leaf": lax.rem(me + d, 8)}

    def x_peer(d):
        return {"blk": lax.rem(bx + d, SIDE) * SIDE + bz, "leaf": me}

    def z_peer(d):
        return {"blk": bx * SIDE + lax.rem(bz + d, SIDE), "leaf": me}

    halves = wide_width // width

    def x_in(w):
        return pltpu.make_async_copy(
            x_hbm.at[:, :, pl.ds(pl.multiple_of(w * wide_width, wide_width), wide_width)],
            xv.at[w], x_sem.at[w])

    def weight_in(i):
        if i == 0:
            return pltpu.make_async_copy(leaf_hbm, leaf, in_sem.at[0])
        if i == 9:
            return pltpu.make_async_copy(row_hbm, row, in_sem.at[9])
        return pltpu.make_async_copy(mix_hbm.at[i - 1], mixes[i - 1], in_sem.at[i])

    weight_in(0).start()
    x_in(0).start()
    for i in range(1, 5):
        weight_in(i).start()
    for w in range(1, chunks // halves):
        x_in(w).start()
    for i in range(5, 10):
        weight_in(i).start()

    barrier = pltpu.get_barrier_semaphore()
    for d in range(1, 8):
        pl.semaphore_signal(barrier, inc=1, device_id=leaf_peer(d), device_id_type=MESH)
    for d in range(1, SIDE):
        pl.semaphore_signal(barrier, inc=1, device_id=x_peer(d), device_id_type=MESH)
        pl.semaphore_signal(barrier, inc=1, device_id=z_peer(d), device_id_type=MESH)

    places = []
    for wanted in range(8):
        found = jnp.int32(0)
        for o in range(8):
            found = found + jnp.where(col_owner[o] == wanted, o, 0)
        places.append(lax.rem(me + 32 - found, 8))

    def keep(value, live):
        row_ids = lax.broadcasted_iota(jnp.int32, value.shape, 0)
        return jnp.where(row_ids < live, value, 0.0).astype(jnp.bfloat16)

    def mix(lhs, top, bottom):
        return dot(lhs, jnp.concatenate([top, bottom], axis=0))

    def pair(ref, p):
        return ref[pl.ds(2 * p, 2)].reshape(2 * rank, 2 * rank)

    def leaf_level(w):
        @pl.loop(0, 4)
        def _(g):
            for u in range(8):
                n = 8 * g + u
                value = lax.dot_general(
                    leaf[n], xv[w, n], (((0,), (0,)), ((), ())),
                    preferred_element_type=jnp.float32)
                ca[n] = keep(value, ranks[0, 0, 0, n])

    def column_level(level, source, target):
        half_i = 2 ** (level - 1)

        @pl.loop(0, 2)
        def _(g):
            for u in range(8):
                p = 8 * g + u
                a = 16 * g + (u // half_i) * (2 * half_i) + u % half_i
                value = mix(pair(mixes[level - 1], p), source[a], source[a + half_i])
                target[2 * p] = keep(value[:rank], ranks[0, level, 0, 2 * p])
                target[2 * p + 1] = keep(value[rank:], ranks[0, level, 0, 2 * p + 1])

    def a2a(c, d, half):
        nodes = pl.ds(2 * parts[half], 2)
        return pltpu.make_async_remote_copy(
            src_ref=send.at[c, d, nodes], dst_ref=recv.at[c, d - 1, nodes],
            send_sem=a_send.at[c, d - 1, half], recv_sem=a_recv.at[c, d - 1, half],
            device_id=leaf_peer(d), device_id_type=MESH)

    def switch_level(w, source):
        waiting = None
        for d in PEERS + (0,):
            s = row_owner[lax.rem(me + d, 8)]
            for j in range(2):
                node = j * 8 + s
                value = mix(pair(t4, node), source[2 * j * 8 + s], source[(2 * j + 1) * 8 + s])
                for e in range(2):
                    kept = keep(value[e * rank:(e + 1) * rank], ranks[0, 4, 0, 2 * node + e])
                    for h in range(halves):
                        send[w * halves + h, d, 2 * e + j] = kept[:, h * width:(h + 1) * width]
            if waiting is not None:
                for half in range(2):
                    a2a(w * halves, waiting, half).start()
            waiting = d
        for h in range(1, halves):
            for half in range(2):
                for d in PEERS:
                    a2a(w * halves + h, d, half).start()

    def phase_a(w):
        x_in(w).wait()

        @pl.when(w == 0)
        def _():
            weight_in(0).wait()

        leaf_level(w)
        for level, source, target in ((1, ca, cb), (2, cb, ca), (3, ca, cb)):
            @pl.when(w == 0)
            def _():
                weight_in(level).wait()

            column_level(level, source, target)

        @pl.when(w == 0)
        def _():
            weight_in(4).wait()
            pl.semaphore_wait(barrier, 7 + 2 * (SIDE - 1))

        switch_level(w, cb)

    def x_first(c, d):
        return pltpu.make_async_remote_copy(
            src_ref=xs.at[c, d], dst_ref=xr.at[c, d - 1],
            send_sem=xs_sem.at[c, d - 1], recv_sem=xr_sem.at[c, d - 1],
            device_id=x_peer(d), device_id_type=MESH)

    def z_first(c, d, half):
        return pltpu.make_async_remote_copy(
            src_ref=zs.at[c, d, pl.ds(2 * half, 2)], dst_ref=zr.at[c, d - 1, pl.ds(2 * half, 2)],
            send_sem=zs_sem.at[c, d - 1, half], recv_sem=zr_sem.at[c, d - 1, half],
            device_id=z_peer(d), device_id_type=MESH)

    def z_second(c, d):
        return pltpu.make_async_remote_copy(
            src_ref=zs2.at[c, d], dst_ref=zr2.at[c, d - 1],
            send_sem=zs2_sem.at[c, d - 1], recv_sem=zr2_sem.at[c, d - 1],
            device_id=z_peer(d), device_id_type=MESH)

    def x_second(c, slot):
        d = turns[slot // 2][slot % 2]
        return pltpu.make_async_remote_copy(
            src_ref=xs2.at[c, slot], dst_ref=xr2.at[c, d - 1],
            send_sem=xs2_sem.at[c, d - 1], recv_sem=xr2_sem.at[c, d - 1],
            device_id=x_peer(d), device_id_type=MESH)

    def arrive(c, d, half):
        owner = lax.rem(me + 8 - d, 8)
        j = col_owner[owner]
        i = parts[half]
        lhs = jnp.concatenate([t5[2 * i * 8 + j], t5[(2 * i + 1) * 8 + j]], axis=0)
        if d == 0:
            nodes = send[c, 0, pl.ds(2 * i, 2)]
        else:
            nodes = recv[c, d - 1, pl.ds(2 * i, 2)]
        value = dot(lhs, nodes.reshape(2 * rank, width))
        for e in range(2):
            c5[2 * i + e, d] = keep(
                value[e * rank:(e + 1) * rank], ranks[0, 5, 0, (2 * i + e) * 8 + j])

    def quarters(c, half):
        pairs = tuple((k, dq, lax.rem(bx + dq, SIDE)) for k, dq in enumerate(turns[half]))
        for k, dq, q in pairs:
            for j in range(4):
                lhs = jnp.concatenate([t6[2 * q * 4 + j], t6[(2 * q + 1) * 4 + j]], axis=0)
                value = mix(lhs, c5[q, places[2 * j]], c5[q, places[2 * j + 1]])
                for e in range(2):
                    c6[k, e * 4 + j] = keep(
                        value[e * rank:(e + 1) * rank], ranks[0, 6, 0, (2 * q + e) * 4 + j])
        for k, dq, q in pairs:
            for i in range(2):
                for j in range(2):
                    base = (2 * q + i) * 4 + j
                    lhs = jnp.concatenate([t7[base], t7[base + 2]], axis=0)
                    value = mix(lhs, c6[k, i * 4 + 2 * j], c6[k, i * 4 + 2 * j + 1])
                    for e in range(2):
                        c7[k, (i * 2 + e) * 2 + j] = keep(
                            value[e * rank:(e + 1) * rank], ranks[0, 7, 0, base + 2 * e])
        for k, dq, q in pairs:
            for i in range(4):
                node = 4 * q + i
                value = mix(pair(t8, node), c7[k, 2 * i], c7[k, 2 * i + 1])
                for e in range(2):
                    c8[k, 2 * i + e] = keep(
                        value[e * rank:(e + 1) * rank], ranks[0, 8, 0, 2 * node + e])
        for k, dq, q in pairs:
            for m in range(4):
                xs[c, dq, m] = dot(row[8 * q + 2 * m], c8[k, 2 * m]).astype(jnp.bfloat16)
        for k, dq, q in pairs:
            for r in range(SIDE):
                m = lax.rem(bz + r, SIDE)
                zs[c, r, 2 * half + k] = dot(
                    row[8 * q + 2 * m + 1], c8[k, 2 * m + 1]).astype(jnp.bfloat16)
        for k, dq, q in pairs:
            if half == 0 or k == 0:
                x_first(c, dq).start()
        for d in (2, 1, 3):
            z_first(c, d, half).start()

    def phase_b(c):
        @pl.when(c == 0)
        def _():
            for i in range(5, 10):
                weight_in(i).wait()

        for half in range(2):
            arrive(c, 0, half)
            for d in (7, 1, 6, 2, 5, 3, 4):
                a2a(c, d, half).wait_recv()
                arrive(c, d, half)
            quarters(c, half)
            if half == 0:
                @pl.when(c >= 1)
                def _():
                    first_sum(c - 1)

    def wide(value):
        return value.astype(jnp.float32)

    def first_sum(c):
        for d in (2, 1, 3):
            x_first(c, d).wait_recv()
        for r in (2, 1, 3, 0):
            m = lax.rem(bz + r, SIDE)
            total = wide(xs[c, 0, m])
            for d in range(SIDE - 1):
                total = total + wide(xr[c, d, m])
            zs2[c, r] = total.astype(jnp.bfloat16)
        for d in (2, 1, 3):
            z_second(c, d).start()
        for d in (2, 1, 3):
            for half in range(2):
                z_first(c, d, half).wait_recv()
        for slot in range(SIDE):
            total = wide(zs[c, 0, slot])
            for d in range(SIDE - 1):
                total = total + wide(zr[c, d, slot])
            xs2[c, slot] = total.astype(jnp.bfloat16)
        for slot in range(SIDE - 1):
            x_second(c, slot).start()

    def last_sum(c):
        columns = pl.ds(pl.multiple_of(c * width, width), width)
        for d in (1, 3, 2):
            z_second(c, d).wait_recv()
        total = wide(zs2[c, 0])
        for d in range(SIDE - 1):
            total = total + wide(zr2[c, d])
        out[pl.ds(0, rank), columns] = total.astype(jnp.bfloat16)
        for slot in range(SIDE - 1):
            x_second(c, slot).wait_recv()
        total = wide(xs2[c, SIDE - 1])
        for d in range(SIDE - 1):
            total = total + wide(xr2[c, d])
        out[pl.ds(rank, rank), columns] = total.astype(jnp.bfloat16)

    @pl.loop(0, chunks // halves)
    def _(w):
        phase_a(w)

    @pl.loop(0, chunks)
    def _(c):
        phase_b(c)

        @pl.when(c >= 1)
        def _():
            last_sum(c - 1)

    first_sum(chunks - 1)
    last_sum(chunks - 1)

    @pl.loop(0, chunks)
    def _(c):
        for d in range(1, 8):
            for half in range(2):
                a2a(c, d, half).wait_send()
        for d in range(1, SIDE):
            x_first(c, d).wait_send()
            for half in range(2):
                z_first(c, d, half).wait_send()
            x_second(c, d - 1).wait_send()
            z_second(c, d).wait_send()


def local(columns_in, leaf_basis, transfers, row_basis, ranks, col_owner, row_owner):
    nodes, leaf_size, rank = leaf_basis.shape[2:]
    sides = columns_in.shape[3]
    levels = transfers.shape[1]
    width = 128
    chunks = sides // width
    wide_width = 2 * width
    bf = jnp.bfloat16
    dma = pltpu.SemaphoreType.DMA
    hbm = pl.BlockSpec(memory_space=pltpu.HBM)
    smem = pl.BlockSpec(memory_space=pltpu.SMEM)
    tile = (rank, width)
    scratch = [pltpu.VMEM((sides // wide_width, nodes, leaf_size, wide_width), bf), pltpu.VMEM((nodes, leaf_size, rank), bf)]
    scratch += [pltpu.VMEM((nodes, rank, 2 * rank), bf)] * levels
    scratch += [pltpu.VMEM((nodes, leaf_size, rank), bf)]
    scratch += [pltpu.VMEM((nodes, rank, wide_width), bf)] * 2
    scratch += [pltpu.VMEM((chunks, 8, 4) + tile, bf), pltpu.VMEM((chunks, 7, 4) + tile, bf)]
    scratch += [pltpu.VMEM((4, 8) + tile, bf)] + [pltpu.VMEM((2, 8) + tile, bf)] * 3
    scratch += [pltpu.VMEM((chunks, 4, 4) + tile, bf)] * 2
    scratch += [pltpu.VMEM((chunks, 3, 4) + tile, bf)] * 2
    scratch += [pltpu.VMEM((chunks, 4) + tile, bf)] * 2
    scratch += [pltpu.VMEM((chunks, 3) + tile, bf)] * 2
    scratch += [dma((10,)), dma((sides // wide_width,)), dma((chunks, 7, 2)), dma((chunks, 7, 2))]
    scratch += [dma((chunks, 3))] * 2 + [dma((chunks, 3, 2))] * 2 + [dma((chunks, 3))] * 4
    share = nodes * leaf_size // lax.axis_size("blk")
    result = pl.pallas_call(
        functools.partial(kernel, chunks, width, wide_width, rank),
        out_shape=jax.ShapeDtypeStruct((share, sides), bf),
        in_specs=[hbm] * 4 + [smem] * 3,
        out_specs=pl.BlockSpec(memory_space=pltpu.VMEM),
        scratch_shapes=scratch,
        compiler_params=pltpu.CompilerParams(
            collective_id=0, has_side_effects=True, vmem_limit_bytes=60 * 1024 * 1024),
        name="block_row",
    )(
        columns_in.reshape(nodes, leaf_size, sides),
        leaf_basis[0, 0],
        transfers[0, :, 0],
        row_basis[0, 0],
        ranks,
        col_owner,
        row_owner,
    )
    return result.reshape(1, share, sides)


def solution(mesh):
    return jax.shard_map(
        local,
        mesh=mesh,
        in_specs=(
            P("blk", "leaf", None, None),
            P("blk", "leaf", None, None, None),
            P("blk", None, "leaf", None, None, None),
            P("blk", "leaf", None, None, None),
            P("blk", None, "leaf", None),
            P(),
            P(),
        ),
        out_specs=P("leaf", "blk", None),
        check_vma=False,
    )
```

```python
import functools

import jax
import jax.numpy as jnp
from jax import lax
from jax.experimental import pallas as pl
from jax.experimental.pallas import tpu as pltpu
from jax.sharding import PartitionSpec as P

MESH = pl.DeviceIdType.MESH
SIDE = 4
PEERS = (4, 3, 5, 2, 6, 1, 7)
ARRIVALS = (7, 1, 6, 2, 5, 3, 4)
AHEAD = 12


def dot(a, b):
    return jnp.dot(a, b, preferred_element_type=jnp.float32)


def kernel(
    chunks, width, wide_width, rank,
    x_hbm, leaf_hbm, mix_hbm, row_hbm, ranks, col_owner, row_owner,
    out,
    xv, leaf, t1, t2, t3, t4, t5, t6, t7, t8, row,
    ca, cb, send, recv, c5, c6, c7, c8,
    xs, zs, xr, zr, xs2, zs2, xr2, zr2,
    in_sem, x_sem,
    a_send, a_recv, xs_sem, xr_sem, zs_sem, zr_sem, xs2_sem, xr2_sem, zs2_sem, zr2_sem,
):
    mixes = (t1, t2, t3, t4, t5, t6, t7, t8)
    me = lax.axis_index("leaf")
    blk = lax.axis_index("blk")
    bx, bz = lax.div(blk, SIDE), lax.rem(blk, SIDE)

    odd = lax.rem(bx, 2)
    turns = ((2, 3 - 2 * odd), (1 + 2 * odd, 0))
    x_pair = lax.div(bx, 2)
    parts = (1 - x_pair, x_pair)

    def leaf_peer(d):
        return {"blk": blk, "leaf": lax.rem(me + d, 8)}

    def x_peer(d):
        return {"blk": lax.rem(bx + d, SIDE) * SIDE + bz, "leaf": me}

    def z_peer(d):
        return {"blk": bx * SIDE + lax.rem(bz + d, SIDE), "leaf": me}

    halves = wide_width // width

    def x_in(w):
        return pltpu.make_async_copy(
            x_hbm.at[:, :, pl.ds(pl.multiple_of(w * wide_width, wide_width), wide_width)],
            xv.at[w], x_sem.at[w])

    def weight_in(i):
        if i == 0:
            return pltpu.make_async_copy(leaf_hbm, leaf, in_sem.at[0])
        if i == 9:
            return pltpu.make_async_copy(row_hbm, row, in_sem.at[9])
        return pltpu.make_async_copy(mix_hbm.at[i - 1], mixes[i - 1], in_sem.at[i])

    weight_in(0).start()
    x_in(0).start()

    barrier = pltpu.get_barrier_semaphore()
    for d in range(1, 8):
        pl.semaphore_signal(barrier, inc=1, device_id=leaf_peer(d), device_id_type=MESH)
    for d in range(1, SIDE):
        pl.semaphore_signal(barrier, inc=1, device_id=x_peer(d), device_id_type=MESH)
        pl.semaphore_signal(barrier, inc=1, device_id=z_peer(d), device_id_type=MESH)

    places = []
    for wanted in range(8):
        found = jnp.int32(0)
        for o in range(8):
            found = found + jnp.where(col_owner[o] == wanted, o, 0)
        places.append(lax.rem(me + 32 - found, 8))

    def keep(value, live):
        row_ids = lax.broadcasted_iota(jnp.int32, value.shape, 0)
        return jnp.where(row_ids < live, value, 0.0).astype(jnp.bfloat16)

    def mix(lhs, top, bottom):
        return dot(lhs, jnp.concatenate([top, bottom], axis=0))

    def pair(ref, p):
        return ref[pl.ds(2 * p, 2)].reshape(2 * rank, 2 * rank)

    def leaf_level(w):
        @pl.loop(0, 4)
        def _(g):
            for u in range(8):
                n = 8 * g + u
                value = lax.dot_general(
                    leaf[n], xv[w, n], (((0,), (0,)), ((), ())),
                    preferred_element_type=jnp.float32)
                ca[n] = keep(value, ranks[0, 0, 0, n])

    def column_level(level, source, target):
        half_i = 2 ** (level - 1)

        @pl.loop(0, 2)
        def _(g):
            for u in range(8):
                p = 8 * g + u
                a = 16 * g + (u // half_i) * (2 * half_i) + u % half_i
                value = mix(pair(mixes[level - 1], p), source[a], source[a + half_i])
                target[2 * p] = keep(value[:rank], ranks[0, level, 0, 2 * p])
                target[2 * p + 1] = keep(value[rank:], ranks[0, level, 0, 2 * p + 1])

    def a2a(c, d, half):
        nodes = pl.ds(2 * parts[half], 2)
        return pltpu.make_async_remote_copy(
            src_ref=send.at[c, d, nodes], dst_ref=recv.at[c, d - 1, nodes],
            send_sem=a_send.at[c, d - 1, half], recv_sem=a_recv.at[c, d - 1, half],
            device_id=leaf_peer(d), device_id_type=MESH)

    def switch_level(w, source):
        waiting = None
        for d in PEERS + (0,):
            s = row_owner[lax.rem(me + d, 8)]
            for j in range(2):
                node = j * 8 + s
                value = mix(pair(t4, node), source[2 * j * 8 + s], source[(2 * j + 1) * 8 + s])
                for e in range(2):
                    kept = keep(value[e * rank:(e + 1) * rank], ranks[0, 4, 0, 2 * node + e])
                    for h in range(halves):
                        send[w * halves + h, d, 2 * e + j] = kept[:, h * width:(h + 1) * width]
            if waiting is not None:
                @pl.when(w == 0)
                def _():
                    a2a(0, waiting, 0).start()

            waiting = d

        @pl.when(w == 0)
        def _():
            for d in ARRIVALS[:AHEAD - 7]:
                a2a(0, d, 1).start()

    def phase_a(w):
        x_in(w).wait()

        @pl.when(w == 0)
        def _():
            weight_in(0).wait()
            weight_in(2).start()
            weight_in(3).start()

        leaf_level(w)
        for level, source, target in ((1, ca, cb), (2, cb, ca), (3, ca, cb)):
            @pl.when(w == 0)
            def _():
                weight_in(level).wait()
                if level == 1:
                    weight_in(4).start()

            column_level(level, source, target)

        @pl.when(w == 0)
        def _():
            weight_in(4).wait()
            for later in range(1, chunks // halves):
                x_in(later).start()
            for i in range(5, 10):
                weight_in(i).start()
            pl.semaphore_wait(barrier, 7 + 2 * (SIDE - 1))

        switch_level(w, cb)

    def follow(c, unit, d):
        if unit < 2:
            a2a(c, d, unit).start()
        else:
            @pl.when(c + unit // 2 < chunks)
            def _():
                a2a(c + unit // 2, d, unit % 2).start()

    def x_first(c, d):
        return pltpu.make_async_remote_copy(
            src_ref=xs.at[c, d], dst_ref=xr.at[c, d - 1],
            send_sem=xs_sem.at[c, d - 1], recv_sem=xr_sem.at[c, d - 1],
            device_id=x_peer(d), device_id_type=MESH)

    def z_first(c, d, half):
        return pltpu.make_async_remote_copy(
            src_ref=zs.at[c, d, pl.ds(2 * half, 2)], dst_ref=zr.at[c, d - 1, pl.ds(2 * half, 2)],
            send_sem=zs_sem.at[c, d - 1, half], recv_sem=zr_sem.at[c, d - 1, half],
            device_id=z_peer(d), device_id_type=MESH)

    def z_second(c, d):
        return pltpu.make_async_remote_copy(
            src_ref=zs2.at[c, d], dst_ref=zr2.at[c, d - 1],
            send_sem=zs2_sem.at[c, d - 1], recv_sem=zr2_sem.at[c, d - 1],
            device_id=z_peer(d), device_id_type=MESH)

    def x_second(c, slot):
        d = turns[slot // 2][slot % 2]
        return pltpu.make_async_remote_copy(
            src_ref=xs2.at[c, slot], dst_ref=xr2.at[c, d - 1],
            send_sem=xs2_sem.at[c, d - 1], recv_sem=xr2_sem.at[c, d - 1],
            device_id=x_peer(d), device_id_type=MESH)

    def arrive(c, d, half):
        owner = lax.rem(me + 8 - d, 8)
        j = col_owner[owner]
        i = parts[half]
        lhs = jnp.concatenate([t5[2 * i * 8 + j], t5[(2 * i + 1) * 8 + j]], axis=0)
        if d == 0:
            nodes = send[c, 0, pl.ds(2 * i, 2)]
        else:
            nodes = recv[c, d - 1, pl.ds(2 * i, 2)]
        value = dot(lhs, nodes.reshape(2 * rank, width))
        for e in range(2):
            c5[2 * i + e, d] = keep(
                value[e * rank:(e + 1) * rank], ranks[0, 5, 0, (2 * i + e) * 8 + j])

    def quarters(c, half):
        pairs = tuple((k, dq, lax.rem(bx + dq, SIDE)) for k, dq in enumerate(turns[half]))
        for k, dq, q in pairs:
            for j in range(4):
                lhs = jnp.concatenate([t6[2 * q * 4 + j], t6[(2 * q + 1) * 4 + j]], axis=0)
                value = mix(lhs, c5[q, places[2 * j]], c5[q, places[2 * j + 1]])
                for e in range(2):
                    c6[k, e * 4 + j] = keep(
                        value[e * rank:(e + 1) * rank], ranks[0, 6, 0, (2 * q + e) * 4 + j])
        for k, dq, q in pairs:
            for i in range(2):
                for j in range(2):
                    base = (2 * q + i) * 4 + j
                    lhs = jnp.concatenate([t7[base], t7[base + 2]], axis=0)
                    value = mix(lhs, c6[k, i * 4 + 2 * j], c6[k, i * 4 + 2 * j + 1])
                    for e in range(2):
                        c7[k, (i * 2 + e) * 2 + j] = keep(
                            value[e * rank:(e + 1) * rank], ranks[0, 7, 0, base + 2 * e])
        for k, dq, q in pairs:
            for i in range(4):
                node = 4 * q + i
                value = mix(pair(t8, node), c7[k, 2 * i], c7[k, 2 * i + 1])
                for e in range(2):
                    c8[k, 2 * i + e] = keep(
                        value[e * rank:(e + 1) * rank], ranks[0, 8, 0, 2 * node + e])
        for k, dq, q in pairs:
            for m in range(4):
                xs[c, dq, m] = dot(row[8 * q + 2 * m], c8[k, 2 * m]).astype(jnp.bfloat16)
        for k, dq, q in pairs:
            for r in range(SIDE):
                m = lax.rem(bz + r, SIDE)
                zs[c, r, 2 * half + k] = dot(
                    row[8 * q + 2 * m + 1], c8[k, 2 * m + 1]).astype(jnp.bfloat16)
        for k, dq, q in pairs:
            if half == 0 or k == 0:
                x_first(c, dq).start()
        for d in (2, 1, 3):
            z_first(c, d, half).start()

    def phase_b(c):
        @pl.when(c == 0)
        def _():
            for i in range(5, 10):
                weight_in(i).wait()

        for half in range(2):
            arrive(c, 0, half)
            for k, d in enumerate(ARRIVALS):
                a2a(c, d, half).wait_recv()
                follow(c, half + (k + AHEAD) // 7, ARRIVALS[(k + AHEAD) % 7])
                arrive(c, d, half)
            quarters(c, half)
            if half == 0:
                @pl.when(c >= 1)
                def _():
                    first_sum(c - 1)

    def wide(value):
        return value.astype(jnp.float32)

    def first_sum(c):
        for d in (2, 1, 3):
            x_first(c, d).wait_recv()
        for r in (2, 1, 3, 0):
            m = lax.rem(bz + r, SIDE)
            total = wide(xs[c, 0, m])
            for d in range(SIDE - 1):
                total = total + wide(xr[c, d, m])
            zs2[c, r] = total.astype(jnp.bfloat16)
        for d in (2, 1, 3):
            z_second(c, d).start()
        for d in (2, 1, 3):
            for half in range(2):
                z_first(c, d, half).wait_recv()
        for slot in range(SIDE):
            total = wide(zs[c, 0, slot])
            for d in range(SIDE - 1):
                total = total + wide(zr[c, d, slot])
            xs2[c, slot] = total.astype(jnp.bfloat16)
        for slot in range(SIDE - 1):
            x_second(c, slot).start()

    def last_sum(c):
        columns = pl.ds(pl.multiple_of(c * width, width), width)
        for d in (1, 3, 2):
            z_second(c, d).wait_recv()
        total = wide(zs2[c, 0])
        for d in range(SIDE - 1):
            total = total + wide(zr2[c, d])
        out[pl.ds(0, rank), columns] = total.astype(jnp.bfloat16)
        for slot in range(SIDE - 1):
            x_second(c, slot).wait_recv()
        total = wide(xs2[c, SIDE - 1])
        for d in range(SIDE - 1):
            total = total + wide(xr2[c, d])
        out[pl.ds(rank, rank), columns] = total.astype(jnp.bfloat16)

    weight_in(1).start()

    @pl.loop(0, chunks // halves)
    def _(w):
        phase_a(w)

    @pl.loop(0, chunks)
    def _(c):
        phase_b(c)

        @pl.when(c >= 1)
        def _():
            last_sum(c - 1)

    first_sum(chunks - 1)
    last_sum(chunks - 1)

    @pl.loop(0, chunks)
    def _(c):
        for d in range(1, 8):
            for half in range(2):
                a2a(c, d, half).wait_send()
        for d in range(1, SIDE):
            x_first(c, d).wait_send()
            for half in range(2):
                z_first(c, d, half).wait_send()
            x_second(c, d - 1).wait_send()
            z_second(c, d).wait_send()


def local(columns_in, leaf_basis, transfers, row_basis, ranks, col_owner, row_owner):
    nodes, leaf_size, rank = leaf_basis.shape[2:]
    sides = columns_in.shape[3]
    levels = transfers.shape[1]
    width = 128
    chunks = sides // width
    wide_width = 2 * width
    bf = jnp.bfloat16
    dma = pltpu.SemaphoreType.DMA
    hbm = pl.BlockSpec(memory_space=pltpu.HBM)
    smem = pl.BlockSpec(memory_space=pltpu.SMEM)
    tile = (rank, width)
    scratch = [pltpu.VMEM((sides // wide_width, nodes, leaf_size, wide_width), bf), pltpu.VMEM((nodes, leaf_size, rank), bf)]
    scratch += [pltpu.VMEM((nodes, rank, 2 * rank), bf)] * levels
    scratch += [pltpu.VMEM((nodes, leaf_size, rank), bf)]
    scratch += [pltpu.VMEM((nodes, rank, wide_width), bf)] * 2
    scratch += [pltpu.VMEM((chunks, 8, 4) + tile, bf), pltpu.VMEM((chunks, 7, 4) + tile, bf)]
    scratch += [pltpu.VMEM((4, 8) + tile, bf)] + [pltpu.VMEM((2, 8) + tile, bf)] * 3
    scratch += [pltpu.VMEM((chunks, 4, 4) + tile, bf)] * 2
    scratch += [pltpu.VMEM((chunks, 3, 4) + tile, bf)] * 2
    scratch += [pltpu.VMEM((chunks, 4) + tile, bf)] * 2
    scratch += [pltpu.VMEM((chunks, 3) + tile, bf)] * 2
    scratch += [dma((10,)), dma((sides // wide_width,)), dma((chunks, 7, 2)), dma((chunks, 7, 2))]
    scratch += [dma((chunks, 3))] * 2 + [dma((chunks, 3, 2))] * 2 + [dma((chunks, 3))] * 4
    share = nodes * leaf_size // lax.axis_size("blk")
    result = pl.pallas_call(
        functools.partial(kernel, chunks, width, wide_width, rank),
        out_shape=jax.ShapeDtypeStruct((share, sides), bf),
        in_specs=[hbm] * 4 + [smem] * 3,
        out_specs=pl.BlockSpec(memory_space=pltpu.VMEM),
        scratch_shapes=scratch,
        compiler_params=pltpu.CompilerParams(
            collective_id=0, has_side_effects=True, vmem_limit_bytes=60 * 1024 * 1024),
        name="block_row",
    )(
        columns_in.reshape(nodes, leaf_size, sides),
        leaf_basis[0, 0],
        transfers[0, :, 0],
        row_basis[0, 0],
        ranks,
        col_owner,
        row_owner,
    )
    return result.reshape(1, share, sides)


def solution(mesh):
    return jax.shard_map(
        local,
        mesh=mesh,
        in_specs=(
            P("blk", "leaf", None, None),
            P("blk", "leaf", None, None, None),
            P("blk", None, "leaf", None, None, None),
            P("blk", "leaf", None, None, None),
            P("blk", None, "leaf", None),
            P(),
            P(),
        ),
        out_specs=P("leaf", "blk", None),
        check_vma=False,
    )
```

```python
import functools

import jax
import jax.numpy as jnp
from jax import lax
from jax.experimental import pallas as pl
from jax.experimental.pallas import tpu as pltpu
from jax.sharding import PartitionSpec as P

MESH = pl.DeviceIdType.MESH
SIDE = 4
PEERS = (4, 3, 5, 2, 6, 1, 7)
ARRIVALS = (7, 1, 6, 2, 5, 3, 4)
AHEAD = 14


def dot(a, b):
    return jnp.dot(a, b, preferred_element_type=jnp.float32)


def kernel(
    chunks, width, rank,
    x_hbm, leaf_hbm, mix_hbm, row_hbm, ranks, col_owner, row_owner,
    out,
    x_head, x_tail, leaf, t1, t2, t3, t4, t5, t6, t7, t8, row,
    head_a, head_b, tail_a, tail_b, send, recv, c5, c6, c7, c8,
    xs, zs, xr, zr, xs2, zs2, xr2, zr2,
    in_sem, x_sem,
    a_send, a_recv, xs_sem, xr_sem, zs_sem, zr_sem, xs2_sem, xr2_sem, zs2_sem, zr2_sem,
):
    mixes = (t1, t2, t3, t4, t5, t6, t7, t8)
    me = lax.axis_index("leaf")
    blk = lax.axis_index("blk")
    bx, bz = lax.div(blk, SIDE), lax.rem(blk, SIDE)

    odd = lax.rem(bx, 2)
    turns = ((2, 3 - 2 * odd), (1 + 2 * odd, 0))
    x_pair = lax.div(bx, 2)
    parts = (1 - x_pair, x_pair)

    def leaf_peer(d):
        return {"blk": blk, "leaf": lax.rem(me + d, 8)}

    def x_peer(d):
        return {"blk": lax.rem(bx + d, SIDE) * SIDE + bz, "leaf": me}

    def z_peer(d):
        return {"blk": bx * SIDE + lax.rem(bz + d, SIDE), "leaf": me}

    def x_in(tail):
        first, count = (1, chunks - 1) if tail else (0, 1)
        return pltpu.make_async_copy(
            x_hbm.at[:, :, pl.ds(first * width, count * width)],
            x_tail if tail else x_head, x_sem.at[int(tail)])

    def weight_in(i):
        if i == 0:
            return pltpu.make_async_copy(leaf_hbm, leaf, in_sem.at[0])
        if i == 9:
            return pltpu.make_async_copy(row_hbm, row, in_sem.at[9])
        return pltpu.make_async_copy(mix_hbm.at[i - 1], mixes[i - 1], in_sem.at[i])

    weight_in(0).start()
    x_in(False).start()

    barrier = pltpu.get_barrier_semaphore()
    for d in range(1, 8):
        pl.semaphore_signal(barrier, inc=1, device_id=leaf_peer(d), device_id_type=MESH)
    for d in range(1, SIDE):
        pl.semaphore_signal(barrier, inc=1, device_id=x_peer(d), device_id_type=MESH)
        pl.semaphore_signal(barrier, inc=1, device_id=z_peer(d), device_id_type=MESH)

    places = []
    for wanted in range(8):
        found = jnp.int32(0)
        for o in range(8):
            found = found + jnp.where(col_owner[o] == wanted, o, 0)
        places.append(lax.rem(me + 32 - found, 8))

    def keep(value, live):
        row_ids = lax.broadcasted_iota(jnp.int32, value.shape, 0)
        return jnp.where(row_ids < live, value, 0.0).astype(jnp.bfloat16)

    def mix(lhs, top, bottom):
        return dot(lhs, jnp.concatenate([top, bottom], axis=0))

    def pair(ref, p):
        return ref[pl.ds(2 * p, 2)].reshape(2 * rank, 2 * rank)

    def leaf_level(source, target):
        @pl.loop(0, 4)
        def _(g):
            for u in range(8):
                n = 8 * g + u
                value = lax.dot_general(
                    leaf[n], source[n], (((0,), (0,)), ((), ())),
                    preferred_element_type=jnp.float32)
                target[n] = keep(value, ranks[0, 0, 0, n])

    def column_level(level, source, target):
        half_i = 2 ** (level - 1)

        @pl.loop(0, 2)
        def _(g):
            for u in range(8):
                p = 8 * g + u
                a = 16 * g + (u // half_i) * (2 * half_i) + u % half_i
                value = mix(pair(mixes[level - 1], p), source[a], source[a + half_i])
                target[2 * p] = keep(value[:rank], ranks[0, level, 0, 2 * p])
                target[2 * p + 1] = keep(value[rank:], ranks[0, level, 0, 2 * p + 1])

    def a2a(c, d, half):
        nodes = pl.ds(2 * parts[half], 2)
        return pltpu.make_async_remote_copy(
            src_ref=send.at[c, d, nodes], dst_ref=recv.at[c, d - 1, nodes],
            send_sem=a_send.at[c, d - 1, half], recv_sem=a_recv.at[c, d - 1, half],
            device_id=leaf_peer(d), device_id_type=MESH)

    def switch_level(tail, source):
        first, count = (1, chunks - 1) if tail else (0, 1)
        waiting = None
        for d in PEERS + (0,):
            s = row_owner[lax.rem(me + d, 8)]
            for j in range(2):
                node = j * 8 + s
                value = mix(pair(t4, node), source[2 * j * 8 + s], source[(2 * j + 1) * 8 + s])
                for e in range(2):
                    kept = keep(value[e * rank:(e + 1) * rank], ranks[0, 4, 0, 2 * node + e])
                    for h in range(count):
                        send[first + h, d, 2 * e + j] = kept[:, h * width:(h + 1) * width]
            if waiting is not None and not tail:
                a2a(0, waiting, 0).start()
            waiting = d
        if not tail:
            for d in ARRIVALS[:AHEAD - 7]:
                a2a(0, d, 1).start()

    def phase_a(tail):
        even, odd_levels = (tail_a, tail_b) if tail else (head_a, head_b)
        x_in(tail).wait()
        if not tail:
            weight_in(0).wait()
            weight_in(2).start()
            weight_in(3).start()
        leaf_level(x_tail if tail else x_head, even)
        for level, source, target in ((1, even, odd_levels), (2, odd_levels, even), (3, even, odd_levels)):
            if not tail:
                weight_in(level).wait()
                if level == 1:
                    weight_in(4).start()
            column_level(level, source, target)
        if not tail:
            weight_in(4).wait()
            x_in(True).start()
            for i in range(5, 10):
                weight_in(i).start()
            pl.semaphore_wait(barrier, 7 + 2 * (SIDE - 1))
        switch_level(tail, odd_levels)

    def follow(c, unit, d):
        if unit < 2:
            a2a(c, d, unit).start()
        else:
            @pl.when(c + unit // 2 < chunks)
            def _():
                a2a(c + unit // 2, d, unit % 2).start()

    def x_first(c, d):
        return pltpu.make_async_remote_copy(
            src_ref=xs.at[c, d], dst_ref=xr.at[c, d - 1],
            send_sem=xs_sem.at[c, d - 1], recv_sem=xr_sem.at[c, d - 1],
            device_id=x_peer(d), device_id_type=MESH)

    def z_first(c, d, half):
        return pltpu.make_async_remote_copy(
            src_ref=zs.at[c, d, pl.ds(2 * half, 2)], dst_ref=zr.at[c, d - 1, pl.ds(2 * half, 2)],
            send_sem=zs_sem.at[c, d - 1, half], recv_sem=zr_sem.at[c, d - 1, half],
            device_id=z_peer(d), device_id_type=MESH)

    def z_second(c, d):
        return pltpu.make_async_remote_copy(
            src_ref=zs2.at[c, d], dst_ref=zr2.at[c, d - 1],
            send_sem=zs2_sem.at[c, d - 1], recv_sem=zr2_sem.at[c, d - 1],
            device_id=z_peer(d), device_id_type=MESH)

    def x_second(c, slot):
        d = turns[slot // 2][slot % 2]
        return pltpu.make_async_remote_copy(
            src_ref=xs2.at[c, slot], dst_ref=xr2.at[c, d - 1],
            send_sem=xs2_sem.at[c, d - 1], recv_sem=xr2_sem.at[c, d - 1],
            device_id=x_peer(d), device_id_type=MESH)

    def arrive(c, d, half):
        owner = lax.rem(me + 8 - d, 8)
        j = col_owner[owner]
        i = parts[half]
        lhs = jnp.concatenate([t5[2 * i * 8 + j], t5[(2 * i + 1) * 8 + j]], axis=0)
        if d == 0:
            nodes = send[c, 0, pl.ds(2 * i, 2)]
        else:
            nodes = recv[c, d - 1, pl.ds(2 * i, 2)]
        value = dot(lhs, nodes.reshape(2 * rank, width))
        for e in range(2):
            c5[2 * i + e, d] = keep(
                value[e * rank:(e + 1) * rank], ranks[0, 5, 0, (2 * i + e) * 8 + j])

    def quarters(c, half):
        pairs = tuple((k, dq, lax.rem(bx + dq, SIDE)) for k, dq in enumerate(turns[half]))
        for k, dq, q in pairs:
            for j in range(4):
                lhs = jnp.concatenate([t6[2 * q * 4 + j], t6[(2 * q + 1) * 4 + j]], axis=0)
                value = mix(lhs, c5[q, places[2 * j]], c5[q, places[2 * j + 1]])
                for e in range(2):
                    c6[k, e * 4 + j] = keep(
                        value[e * rank:(e + 1) * rank], ranks[0, 6, 0, (2 * q + e) * 4 + j])
        for k, dq, q in pairs:
            for i in range(2):
                for j in range(2):
                    base = (2 * q + i) * 4 + j
                    lhs = jnp.concatenate([t7[base], t7[base + 2]], axis=0)
                    value = mix(lhs, c6[k, i * 4 + 2 * j], c6[k, i * 4 + 2 * j + 1])
                    for e in range(2):
                        c7[k, (i * 2 + e) * 2 + j] = keep(
                            value[e * rank:(e + 1) * rank], ranks[0, 7, 0, base + 2 * e])
        for k, dq, q in pairs:
            for i in range(4):
                node = 4 * q + i
                value = mix(pair(t8, node), c7[k, 2 * i], c7[k, 2 * i + 1])
                for e in range(2):
                    c8[k, 2 * i + e] = keep(
                        value[e * rank:(e + 1) * rank], ranks[0, 8, 0, 2 * node + e])
        for k, dq, q in pairs:
            for m in range(4):
                xs[c, dq, m] = dot(row[8 * q + 2 * m], c8[k, 2 * m]).astype(jnp.bfloat16)
        for k, dq, q in pairs:
            for r in range(SIDE):
                m = lax.rem(bz + r, SIDE)
                zs[c, r, 2 * half + k] = dot(
                    row[8 * q + 2 * m + 1], c8[k, 2 * m + 1]).astype(jnp.bfloat16)
            if half == 0 or k == 0:
                x_first(c, dq).start()
        for d in (2, 1, 3):
            z_first(c, d, half).start()

    def phase_b(c):
        @pl.when(c == 0)
        def _():
            for i in range(5, 10):
                weight_in(i).wait()

        for half in range(2):
            arrive(c, 0, half)
            for k, d in enumerate(ARRIVALS):
                a2a(c, d, half).wait_recv()
                follow(c, half + (k + AHEAD) // 7, ARRIVALS[(k + AHEAD) % 7])
                arrive(c, d, half)
            quarters(c, half)
            if half == 0:
                @pl.when(c >= 1)
                def _():
                    first_sum(c - 1)

    def wide(value):
        return value.astype(jnp.float32)

    def x_total(c, m):
        total = wide(xs[c, 0, m])
        for d in range(SIDE - 1):
            total = total + wide(xr[c, d, m])
        return total.astype(jnp.bfloat16)

    def z_total(c, slot):
        total = wide(zs[c, 0, slot])
        for d in range(SIDE - 1):
            total = total + wide(zr[c, d, slot])
        return total.astype(jnp.bfloat16)

    def first_sum(c):
        for d in (2, 1, 3):
            z_first(c, d, 0).wait_recv()
        for slot in range(2):
            xs2[c, slot] = z_total(c, slot)
        for d in (2, 1, 3):
            x_first(c, d).wait_recv()
        ready = None
        for r in (2, 1, 3):
            zs2[c, r] = x_total(c, lax.rem(bz + r, SIDE))
            if ready is None:
                for slot in range(2):
                    x_second(c, slot).start()
            else:
                z_second(c, ready).start()
            ready = r
        for d in (2, 1, 3):
            z_first(c, d, 1).wait_recv()
        xs2[c, 2] = z_total(c, 2)
        z_second(c, ready).start()
        zs2[c, 0] = x_total(c, bz)
        x_second(c, 2).start()
        xs2[c, 3] = z_total(c, 3)

    def last_sum(c):
        columns = pl.ds(pl.multiple_of(c * width, width), width)
        for d in (1, 3, 2):
            z_second(c, d).wait_recv()
        total = wide(zs2[c, 0])
        for d in range(SIDE - 1):
            total = total + wide(zr2[c, d])
        out[pl.ds(0, rank), columns] = total.astype(jnp.bfloat16)
        for slot in range(SIDE - 1):
            x_second(c, slot).wait_recv()
        total = wide(xs2[c, SIDE - 1])
        for d in range(SIDE - 1):
            total = total + wide(xr2[c, d])
        out[pl.ds(rank, rank), columns] = total.astype(jnp.bfloat16)

    weight_in(1).start()

    phase_a(False)
    phase_a(True)

    @pl.loop(0, chunks)
    def _(c):
        phase_b(c)

        @pl.when(c >= 1)
        def _():
            last_sum(c - 1)

    first_sum(chunks - 1)
    last_sum(chunks - 1)

    @pl.loop(0, chunks)
    def _(c):
        for d in range(1, 8):
            for half in range(2):
                a2a(c, d, half).wait_send()
        for d in range(1, SIDE):
            x_first(c, d).wait_send()
            for half in range(2):
                z_first(c, d, half).wait_send()
            x_second(c, d - 1).wait_send()
            z_second(c, d).wait_send()


def local(columns_in, leaf_basis, transfers, row_basis, ranks, col_owner, row_owner):
    nodes, leaf_size, rank = leaf_basis.shape[2:]
    sides = columns_in.shape[3]
    levels = transfers.shape[1]
    width = 128
    chunks = sides // width
    rest = sides - width
    bf = jnp.bfloat16
    dma = pltpu.SemaphoreType.DMA
    hbm = pl.BlockSpec(memory_space=pltpu.HBM)
    smem = pl.BlockSpec(memory_space=pltpu.SMEM)
    tile = (rank, width)
    scratch = [pltpu.VMEM((nodes, leaf_size, width), bf), pltpu.VMEM((nodes, leaf_size, rest), bf)]
    scratch += [pltpu.VMEM((nodes, leaf_size, rank), bf)]
    scratch += [pltpu.VMEM((nodes, rank, 2 * rank), bf)] * levels
    scratch += [pltpu.VMEM((nodes, leaf_size, rank), bf)]
    scratch += [pltpu.VMEM((nodes, rank, width), bf)] * 2 + [pltpu.VMEM((nodes, rank, rest), bf)] * 2
    scratch += [pltpu.VMEM((chunks, 8, 4) + tile, bf), pltpu.VMEM((chunks, 7, 4) + tile, bf)]
    scratch += [pltpu.VMEM((4, 8) + tile, bf)] + [pltpu.VMEM((2, 8) + tile, bf)] * 3
    scratch += [pltpu.VMEM((chunks, 4, 4) + tile, bf)] * 2
    scratch += [pltpu.VMEM((chunks, 3, 4) + tile, bf)] * 2
    scratch += [pltpu.VMEM((chunks, 4) + tile, bf)] * 2
    scratch += [pltpu.VMEM((chunks, 3) + tile, bf)] * 2
    scratch += [dma((10,)), dma((2,)), dma((chunks, 7, 2)), dma((chunks, 7, 2))]
    scratch += [dma((chunks, 3))] * 2 + [dma((chunks, 3, 2))] * 2 + [dma((chunks, 3))] * 4
    share = nodes * leaf_size // lax.axis_size("blk")
    result = pl.pallas_call(
        functools.partial(kernel, chunks, width, rank),
        out_shape=jax.ShapeDtypeStruct((share, sides), bf),
        in_specs=[hbm] * 4 + [smem] * 3,
        out_specs=pl.BlockSpec(memory_space=pltpu.VMEM),
        scratch_shapes=scratch,
        compiler_params=pltpu.CompilerParams(
            collective_id=0, has_side_effects=True, vmem_limit_bytes=60 * 1024 * 1024),
        name="block_row",
    )(
        columns_in.reshape(nodes, leaf_size, sides),
        leaf_basis[0, 0],
        transfers[0, :, 0],
        row_basis[0, 0],
        ranks,
        col_owner,
        row_owner,
    )
    return result.reshape(1, share, sides)


def solution(mesh):
    return jax.shard_map(
        local,
        mesh=mesh,
        in_specs=(
            P("blk", "leaf", None, None),
            P("blk", "leaf", None, None, None),
            P("blk", None, "leaf", None, None, None),
            P("blk", "leaf", None, None, None),
            P("blk", None, "leaf", None),
            P(),
            P(),
        ),
        out_specs=P("leaf", "blk", None),
        check_vma=False,
    )
```

```python
import functools

import jax
import jax.numpy as jnp
from jax import lax
from jax.experimental import pallas as pl
from jax.experimental.pallas import tpu as pltpu
from jax.sharding import PartitionSpec as P

MESH = pl.DeviceIdType.MESH
SIDE = 4
PEERS = (4, 3, 5, 2, 6, 1, 7)
ARRIVALS = (7, 1, 6, 2, 5, 3, 4)
AHEAD = 14


def dot(a, b):
    return jnp.dot(a, b, preferred_element_type=jnp.float32)


def kernel(
    chunks, width, rank,
    x_hbm, leaf_hbm, mix_hbm, row_hbm, ranks, col_owner, row_owner,
    out,
    x_head, x_tail, leaf, t1, t2, t3, t4, t5, t6, t7, t8, row,
    head_a, head_b, tail_a, tail_b, send, recv, c5, c6, c7, c8,
    xs, zs, xr, zr, xs2, zs2, xr2, zr2,
    in_sem, x_sem,
    a_send, a_recv, xs_sem, xr_sem, zs_sem, zr_sem, xs2_sem, xr2_sem, zs2_sem, zr2_sem,
):
    mixes = (t1, t2, t3, t4, t5, t6, t7, t8)
    me = lax.axis_index("leaf")
    blk = lax.axis_index("blk")
    bx, bz = lax.div(blk, SIDE), lax.rem(blk, SIDE)

    odd = lax.rem(bx, 2)
    turns = ((2, 3 - 2 * odd), (1 + 2 * odd, 0))
    x_pair = lax.div(bx, 2)
    parts = (1 - x_pair, x_pair)

    def leaf_peer(d):
        return {"blk": blk, "leaf": lax.rem(me + d, 8)}

    def x_peer(d):
        return {"blk": lax.rem(bx + d, SIDE) * SIDE + bz, "leaf": me}

    def z_peer(d):
        return {"blk": bx * SIDE + lax.rem(bz + d, SIDE), "leaf": me}

    def x_in(tail):
        first, count = (1, chunks - 1) if tail else (0, 1)
        return pltpu.make_async_copy(
            x_hbm.at[:, :, pl.ds(first * width, count * width)],
            x_tail if tail else x_head, x_sem.at[int(tail)])

    def weight_in(i):
        if i == 0:
            return pltpu.make_async_copy(leaf_hbm, leaf, in_sem.at[0])
        if i == 9:
            return pltpu.make_async_copy(row_hbm, row, in_sem.at[9])
        return pltpu.make_async_copy(mix_hbm.at[i - 1], mixes[i - 1], in_sem.at[i])

    weight_in(0).start()
    x_in(False).start()

    barrier = pltpu.get_barrier_semaphore()
    for d in range(1, 8):
        pl.semaphore_signal(barrier, inc=1, device_id=leaf_peer(d), device_id_type=MESH)
    for d in range(1, SIDE):
        pl.semaphore_signal(barrier, inc=1, device_id=x_peer(d), device_id_type=MESH)
        pl.semaphore_signal(barrier, inc=1, device_id=z_peer(d), device_id_type=MESH)

    places = []
    for wanted in range(8):
        found = jnp.int32(0)
        for o in range(8):
            found = found + jnp.where(col_owner[o] == wanted, o, 0)
        places.append(lax.rem(me + 32 - found, 8))

    def keep(value, live):
        row_ids = lax.broadcasted_iota(jnp.int32, value.shape, 0)
        return jnp.where(row_ids < live, value, 0.0).astype(jnp.bfloat16)

    def mix(lhs, top, bottom):
        return dot(lhs, jnp.concatenate([top, bottom], axis=0))

    def pair(ref, p):
        return ref[pl.ds(2 * p, 2)].reshape(2 * rank, 2 * rank)

    def leaf_level(source, target):
        @pl.loop(0, 4)
        def _(g):
            for u in range(8):
                n = 8 * g + u
                value = lax.dot_general(
                    leaf[n], source[n], (((0,), (0,)), ((), ())),
                    preferred_element_type=jnp.float32)
                target[n] = keep(value, ranks[0, 0, 0, n])

    def column_level(level, source, target):
        half_i = 2 ** (level - 1)

        @pl.loop(0, 2)
        def _(g):
            for u in range(8):
                p = 8 * g + u
                a = 16 * g + (u // half_i) * (2 * half_i) + u % half_i
                value = mix(pair(mixes[level - 1], p), source[a], source[a + half_i])
                target[2 * p] = keep(value[:rank], ranks[0, level, 0, 2 * p])
                target[2 * p + 1] = keep(value[rank:], ranks[0, level, 0, 2 * p + 1])

    def a2a(c, d, half):
        nodes = pl.ds(2 * parts[half], 2)
        return pltpu.make_async_remote_copy(
            src_ref=send.at[c, d, nodes], dst_ref=recv.at[c, d - 1, nodes],
            send_sem=a_send.at[c, d - 1, half], recv_sem=a_recv.at[c, d - 1, half],
            device_id=leaf_peer(d), device_id_type=MESH)

    def switch_level(tail, source):
        first, count = (1, chunks - 1) if tail else (0, 1)
        waiting = None
        for d in PEERS + (0,):
            s = row_owner[lax.rem(me + d, 8)]
            for j in range(2):
                node = j * 8 + s
                value = mix(pair(t4, node), source[2 * j * 8 + s], source[(2 * j + 1) * 8 + s])
                for e in range(2):
                    kept = keep(value[e * rank:(e + 1) * rank], ranks[0, 4, 0, 2 * node + e])
                    for h in range(count):
                        send[first + h, d, 2 * e + j] = kept[:, h * width:(h + 1) * width]
            if waiting is not None and not tail:
                a2a(0, waiting, 0).start()
            waiting = d
        if not tail:
            for d in ARRIVALS[:AHEAD - 7]:
                a2a(0, d, 1).start()

    def phase_a(tail):
        even, odd_levels = (tail_a, tail_b) if tail else (head_a, head_b)
        x_in(tail).wait()
        if not tail:
            weight_in(0).wait()
            weight_in(2).start()
            weight_in(3).start()
        leaf_level(x_tail if tail else x_head, even)
        for level, source, target in ((1, even, odd_levels), (2, odd_levels, even), (3, even, odd_levels)):
            if not tail:
                weight_in(level).wait()
                if level == 1:
                    weight_in(4).start()
            column_level(level, source, target)
        if not tail:
            weight_in(4).wait()
            x_in(True).start()
            for i in range(5, 10):
                weight_in(i).start()
            pl.semaphore_wait(barrier, 7 + 2 * (SIDE - 1))
        switch_level(tail, odd_levels)

    def follow(c, unit, d):
        if unit < 2:
            a2a(c, d, unit).start()
        else:
            @pl.when(c + unit // 2 < chunks)
            def _():
                a2a(c + unit // 2, d, unit % 2).start()

    def x_first(c, d):
        return pltpu.make_async_remote_copy(
            src_ref=xs.at[c, d], dst_ref=xr.at[c, d - 1],
            send_sem=xs_sem.at[c, d - 1], recv_sem=xr_sem.at[c, d - 1],
            device_id=x_peer(d), device_id_type=MESH)

    def z_first(c, d, half):
        return pltpu.make_async_remote_copy(
            src_ref=zs.at[c, d, pl.ds(2 * half, 2)], dst_ref=zr.at[c, d - 1, pl.ds(2 * half, 2)],
            send_sem=zs_sem.at[c, d - 1, half], recv_sem=zr_sem.at[c, d - 1, half],
            device_id=z_peer(d), device_id_type=MESH)

    def z_second(c, d):
        return pltpu.make_async_remote_copy(
            src_ref=zs2.at[c, d], dst_ref=zr2.at[c, d - 1],
            send_sem=zs2_sem.at[c, d - 1], recv_sem=zr2_sem.at[c, d - 1],
            device_id=z_peer(d), device_id_type=MESH)

    def x_second(c, slot):
        d = turns[slot // 2][slot % 2]
        return pltpu.make_async_remote_copy(
            src_ref=xs2.at[c, slot], dst_ref=xr2.at[c, d - 1],
            send_sem=xs2_sem.at[c, d - 1], recv_sem=xr2_sem.at[c, d - 1],
            device_id=x_peer(d), device_id_type=MESH)

    def arrive(c, d, half):
        owner = lax.rem(me + 8 - d, 8)
        j = col_owner[owner]
        i = parts[half]
        lhs = jnp.concatenate([t5[2 * i * 8 + j], t5[(2 * i + 1) * 8 + j]], axis=0)
        if d == 0:
            nodes = send[c, 0, pl.ds(2 * i, 2)]
        else:
            nodes = recv[c, d - 1, pl.ds(2 * i, 2)]
        value = dot(lhs, nodes.reshape(2 * rank, width))
        for e in range(2):
            c5[2 * i + e, d] = keep(
                value[e * rank:(e + 1) * rank], ranks[0, 5, 0, (2 * i + e) * 8 + j])

    def quarters(c, half):
        pairs = tuple((k, dq, lax.rem(bx + dq, SIDE)) for k, dq in enumerate(turns[half]))
        for k, dq, q in pairs:
            for j in range(4):
                lhs = jnp.concatenate([t6[2 * q * 4 + j], t6[(2 * q + 1) * 4 + j]], axis=0)
                value = mix(lhs, c5[q, places[2 * j]], c5[q, places[2 * j + 1]])
                for e in range(2):
                    c6[k, e * 4 + j] = keep(
                        value[e * rank:(e + 1) * rank], ranks[0, 6, 0, (2 * q + e) * 4 + j])
        for k, dq, q in pairs:
            for i in range(2):
                for j in range(2):
                    base = (2 * q + i) * 4 + j
                    lhs = jnp.concatenate([t7[base], t7[base + 2]], axis=0)
                    value = mix(lhs, c6[k, i * 4 + 2 * j], c6[k, i * 4 + 2 * j + 1])
                    for e in range(2):
                        c7[k, (i * 2 + e) * 2 + j] = keep(
                            value[e * rank:(e + 1) * rank], ranks[0, 7, 0, base + 2 * e])
        for k, dq, q in pairs:
            for i in range(4):
                node = 4 * q + i
                value = mix(pair(t8, node), c7[k, 2 * i], c7[k, 2 * i + 1])
                for e in range(2):
                    c8[k, 2 * i + e] = keep(
                        value[e * rank:(e + 1) * rank], ranks[0, 8, 0, 2 * node + e])
        for k, dq, q in pairs:
            for m in range(4):
                xs[c, dq, m] = dot(row[8 * q + 2 * m], c8[k, 2 * m]).astype(jnp.bfloat16)
        for k, dq, q in pairs:
            for r in range(SIDE):
                m = lax.rem(bz + r, SIDE)
                zs[c, r, 2 * half + k] = dot(
                    row[8 * q + 2 * m + 1], c8[k, 2 * m + 1]).astype(jnp.bfloat16)
            if half == 0 or k == 0:
                x_first(c, dq).start()
        for d in (2, 1, 3):
            z_first(c, d, half).start()

    def phase_b(c):
        @pl.when(c == 0)
        def _():
            for i in range(5, 10):
                weight_in(i).wait()

        for half in range(2):
            arrive(c, 0, half)
            for k, d in enumerate(ARRIVALS):
                a2a(c, d, half).wait_recv()
                follow(c, half + (k + AHEAD) // 7, ARRIVALS[(k + AHEAD) % 7])
                arrive(c, d, half)
            quarters(c, half)
            if half == 0:
                @pl.when(c == chunks - 1)
                def _():
                    first_sum(c - 1)

    def wide(value):
        return value.astype(jnp.float32)

    def x_total(c, m):
        total = wide(xs[c, 0, m])
        for d in range(SIDE - 1):
            total = total + wide(xr[c, d, m])
        return total.astype(jnp.bfloat16)

    def z_total(c, slot):
        total = wide(zs[c, 0, slot])
        for d in range(SIDE - 1):
            total = total + wide(zr[c, d, slot])
        return total.astype(jnp.bfloat16)

    def first_sum(c):
        for d in (2, 1, 3):
            z_first(c, d, 0).wait_recv()
        for slot in range(2):
            xs2[c, slot] = z_total(c, slot)
        for d in (2, 1, 3):
            x_first(c, d).wait_recv()
        ready = None
        for r in (2, 1, 3):
            zs2[c, r] = x_total(c, lax.rem(bz + r, SIDE))
            if ready is None:
                for slot in range(2):
                    x_second(c, slot).start()
            else:
                z_second(c, ready).start()
            ready = r
        for d in (2, 1, 3):
            z_first(c, d, 1).wait_recv()
        xs2[c, 2] = z_total(c, 2)
        z_second(c, ready).start()
        zs2[c, 0] = x_total(c, bz)
        x_second(c, 2).start()
        xs2[c, 3] = z_total(c, 3)

    def last_sum(c):
        columns = pl.ds(pl.multiple_of(c * width, width), width)
        for d in (1, 3, 2):
            z_second(c, d).wait_recv()
        total = wide(zs2[c, 0])
        for d in range(SIDE - 1):
            total = total + wide(zr2[c, d])
        out[pl.ds(0, rank), columns] = total.astype(jnp.bfloat16)
        for slot in range(SIDE - 1):
            x_second(c, slot).wait_recv()
        total = wide(xs2[c, SIDE - 1])
        for d in range(SIDE - 1):
            total = total + wide(xr2[c, d])
        out[pl.ds(rank, rank), columns] = total.astype(jnp.bfloat16)

    weight_in(1).start()

    def drain(c):
        for d in range(1, 8):
            for half in range(2):
                a2a(c, d, half).wait_send()
        for d in range(1, SIDE):
            x_first(c, d).wait_send()
            for half in range(2):
                z_first(c, d, half).wait_send()
            x_second(c, d - 1).wait_send()
            z_second(c, d).wait_send()

    phase_a(False)
    phase_a(True)

    @pl.loop(0, chunks)
    def _(c):
        phase_b(c)

        @pl.when((c >= 1) & (c < chunks - 1))
        def _():
            first_sum(c - 1)

        @pl.when(c >= 2)
        def _():
            last_sum(c - 2)

    first_sum(chunks - 1)
    last_sum(chunks - 2)

    @pl.loop(0, chunks - 1)
    def _(c):
        drain(c)

    last_sum(chunks - 1)

    drain(chunks - 1)


def local(columns_in, leaf_basis, transfers, row_basis, ranks, col_owner, row_owner):
    nodes, leaf_size, rank = leaf_basis.shape[2:]
    sides = columns_in.shape[3]
    levels = transfers.shape[1]
    width = 128
    chunks = sides // width
    rest = sides - width
    bf = jnp.bfloat16
    dma = pltpu.SemaphoreType.DMA
    hbm = pl.BlockSpec(memory_space=pltpu.HBM)
    smem = pl.BlockSpec(memory_space=pltpu.SMEM)
    tile = (rank, width)
    scratch = [pltpu.VMEM((nodes, leaf_size, width), bf), pltpu.VMEM((nodes, leaf_size, rest), bf)]
    scratch += [pltpu.VMEM((nodes, leaf_size, rank), bf)]
    scratch += [pltpu.VMEM((nodes, rank, 2 * rank), bf)] * levels
    scratch += [pltpu.VMEM((nodes, leaf_size, rank), bf)]
    scratch += [pltpu.VMEM((nodes, rank, width), bf)] * 2 + [pltpu.VMEM((nodes, rank, rest), bf)] * 2
    scratch += [pltpu.VMEM((chunks, 8, 4) + tile, bf), pltpu.VMEM((chunks, 7, 4) + tile, bf)]
    scratch += [pltpu.VMEM((4, 8) + tile, bf)] + [pltpu.VMEM((2, 8) + tile, bf)] * 3
    scratch += [pltpu.VMEM((chunks, 4, 4) + tile, bf)] * 2
    scratch += [pltpu.VMEM((chunks, 3, 4) + tile, bf)] * 2
    scratch += [pltpu.VMEM((chunks, 4) + tile, bf)] * 2
    scratch += [pltpu.VMEM((chunks, 3) + tile, bf)] * 2
    scratch += [dma((10,)), dma((2,)), dma((chunks, 7, 2)), dma((chunks, 7, 2))]
    scratch += [dma((chunks, 3))] * 2 + [dma((chunks, 3, 2))] * 2 + [dma((chunks, 3))] * 4
    share = nodes * leaf_size // lax.axis_size("blk")
    result = pl.pallas_call(
        functools.partial(kernel, chunks, width, rank),
        out_shape=jax.ShapeDtypeStruct((share, sides), bf),
        in_specs=[hbm] * 4 + [smem] * 3,
        out_specs=pl.BlockSpec(memory_space=pltpu.VMEM),
        scratch_shapes=scratch,
        compiler_params=pltpu.CompilerParams(
            collective_id=0, has_side_effects=True, vmem_limit_bytes=60 * 1024 * 1024),
        name="block_row",
    )(
        columns_in.reshape(nodes, leaf_size, sides),
        leaf_basis[0, 0],
        transfers[0, :, 0],
        row_basis[0, 0],
        ranks,
        col_owner,
        row_owner,
    )
    return result.reshape(1, share, sides)


def solution(mesh):
    return jax.shard_map(
        local,
        mesh=mesh,
        in_specs=(
            P("blk", "leaf", None, None),
            P("blk", "leaf", None, None, None),
            P("blk", None, "leaf", None, None, None),
            P("blk", "leaf", None, None, None),
            P("blk", None, "leaf", None),
            P(),
            P(),
        ),
        out_specs=P("leaf", "blk", None),
        check_vma=False,
    )
```

```python
import functools

import jax
import jax.numpy as jnp
from jax import lax
from jax.experimental import pallas as pl
from jax.experimental.pallas import tpu as pltpu
from jax.sharding import PartitionSpec as P

MESH = pl.DeviceIdType.MESH
SIDE = 4
PEERS = (4, 3, 5, 2, 6, 1, 7)
ARRIVALS = (7, 1, 6, 2, 5, 3, 4)
AHEAD = 14


def dot(a, b):
    return jnp.dot(a, b, preferred_element_type=jnp.float32)


def kernel(
    chunks, width, rank,
    x_hbm, leaf_hbm, mix_hbm, row_hbm, ranks, col_owner, row_owner,
    out,
    x_head, x_tail, leaf, t1, t2, t3, t4, t5, t6, t7, t8, row,
    head_a, head_b, tail_a, tail_b, send, recv, c5, c6, c7, c8,
    xs, zs, xr, zr, xs2, zs2, xr2, zr2,
    in_sem, x_sem,
    a_send, a_recv, xs_sem, xr_sem, zs_sem, zr_sem, xs2_sem, xr2_sem, zs2_sem, zr2_sem,
):
    mixes = (t1, t2, t3, t4, t5, t6, t7, t8)
    me = lax.axis_index("leaf")
    blk = lax.axis_index("blk")
    bx, bz = lax.div(blk, SIDE), lax.rem(blk, SIDE)

    odd = lax.rem(bx, 2)
    turns = ((2, 3 - 2 * odd), (1 + 2 * odd, 0))
    x_pair = lax.div(bx, 2)
    parts = (1 - x_pair, x_pair)

    def leaf_peer(d):
        return {"blk": blk, "leaf": lax.rem(me + d, 8)}

    def x_peer(d):
        return {"blk": lax.rem(bx + d, SIDE) * SIDE + bz, "leaf": me}

    def z_peer(d):
        return {"blk": bx * SIDE + lax.rem(bz + d, SIDE), "leaf": me}

    def x_in(tail):
        first, count = (1, chunks - 1) if tail else (0, 1)
        return pltpu.make_async_copy(
            x_hbm.at[:, :, pl.ds(first * width, count * width)],
            x_tail if tail else x_head, x_sem.at[int(tail)])

    def weight_in(i):
        if i == 0:
            return pltpu.make_async_copy(leaf_hbm, leaf, in_sem.at[0])
        if i == 9:
            return pltpu.make_async_copy(row_hbm, row, in_sem.at[9])
        return pltpu.make_async_copy(mix_hbm.at[i - 1], mixes[i - 1], in_sem.at[i])

    weight_in(0).start()
    x_in(False).start()

    barrier = pltpu.get_barrier_semaphore()
    for d in range(1, 8):
        pl.semaphore_signal(barrier, inc=1, device_id=leaf_peer(d), device_id_type=MESH)
    for d in range(1, SIDE):
        pl.semaphore_signal(barrier, inc=1, device_id=x_peer(d), device_id_type=MESH)
        pl.semaphore_signal(barrier, inc=1, device_id=z_peer(d), device_id_type=MESH)

    places = []
    for wanted in range(8):
        found = jnp.int32(0)
        for o in range(8):
            found = found + jnp.where(col_owner[o] == wanted, o, 0)
        places.append(lax.rem(me + 32 - found, 8))

    def keep(value, live):
        row_ids = lax.broadcasted_iota(jnp.int32, value.shape, 0)
        return jnp.where(row_ids < live, value, 0.0).astype(jnp.bfloat16)

    def mix(lhs, top, bottom):
        return dot(lhs, jnp.concatenate([top, bottom], axis=0))

    def pair(ref, p):
        return ref[pl.ds(2 * p, 2)].reshape(2 * rank, 2 * rank)

    def leaf_level(source, target):
        @pl.loop(0, 4)
        def _(g):
            for u in range(8):
                n = 8 * g + u
                value = lax.dot_general(
                    leaf[n], source[n], (((0,), (0,)), ((), ())),
                    preferred_element_type=jnp.float32)
                target[n] = keep(value, ranks[0, 0, 0, n])

    def column_level(level, source, target):
        half_i = 2 ** (level - 1)

        @pl.loop(0, 2)
        def _(g):
            for u in range(8):
                p = 8 * g + u
                a = 16 * g + (u // half_i) * (2 * half_i) + u % half_i
                value = mix(pair(mixes[level - 1], p), source[a], source[a + half_i])
                target[2 * p] = keep(value[:rank], ranks[0, level, 0, 2 * p])
                target[2 * p + 1] = keep(value[rank:], ranks[0, level, 0, 2 * p + 1])

    def a2a(c, d, half):
        nodes = pl.ds(2 * parts[half], 2)
        return pltpu.make_async_remote_copy(
            src_ref=send.at[c, d, nodes], dst_ref=recv.at[c, d - 1, nodes],
            send_sem=a_send.at[c, d - 1, half], recv_sem=a_recv.at[c, d - 1, half],
            device_id=leaf_peer(d), device_id_type=MESH)

    def switch_level(tail, source):
        first, count = (1, chunks - 1) if tail else (0, 1)
        waiting = None
        for d in PEERS + (0,):
            s = row_owner[lax.rem(me + d, 8)]
            for j in range(2):
                node = j * 8 + s
                value = mix(pair(t4, node), source[2 * j * 8 + s], source[(2 * j + 1) * 8 + s])
                for e in range(2):
                    kept = keep(value[e * rank:(e + 1) * rank], ranks[0, 4, 0, 2 * node + e])
                    for h in range(count):
                        send[first + h, d, 2 * e + j] = kept[:, h * width:(h + 1) * width]
            if waiting is not None and not tail:
                a2a(0, waiting, 0).start()
            waiting = d
        if not tail:
            for d in ARRIVALS[:AHEAD - 7]:
                a2a(0, d, 1).start()

    def phase_a(tail):
        even, odd_levels = (tail_a, tail_b) if tail else (head_a, head_b)
        x_in(tail).wait()
        if not tail:
            weight_in(0).wait()
            weight_in(2).start()
            weight_in(3).start()
        leaf_level(x_tail if tail else x_head, even)
        for level, source, target in ((1, even, odd_levels), (2, odd_levels, even), (3, even, odd_levels)):
            if not tail:
                weight_in(level).wait()
                if level == 1:
                    weight_in(4).start()
            column_level(level, source, target)
        if not tail:
            weight_in(4).wait()
            x_in(True).start()
            for i in range(5, 10):
                weight_in(i).start()
            pl.semaphore_wait(barrier, 7 + 2 * (SIDE - 1))
        switch_level(tail, odd_levels)

    def follow(c, unit, d):
        if unit < 2:
            a2a(c, d, unit).start()
        else:
            @pl.when(c + unit // 2 < chunks)
            def _():
                a2a(c + unit // 2, d, unit % 2).start()

    def x_first(c, d):
        return pltpu.make_async_remote_copy(
            src_ref=xs.at[c, d], dst_ref=xr.at[c, d - 1],
            send_sem=xs_sem.at[c, d - 1], recv_sem=xr_sem.at[c, d - 1],
            device_id=x_peer(d), device_id_type=MESH)

    def z_first(c, d, half):
        return pltpu.make_async_remote_copy(
            src_ref=zs.at[c, d, pl.ds(2 * half, 2)], dst_ref=zr.at[c, d - 1, pl.ds(2 * half, 2)],
            send_sem=zs_sem.at[c, d - 1, half], recv_sem=zr_sem.at[c, d - 1, half],
            device_id=z_peer(d), device_id_type=MESH)

    def z_second(c, d):
        return pltpu.make_async_remote_copy(
            src_ref=zs2.at[c, d], dst_ref=zr2.at[c, d - 1],
            send_sem=zs2_sem.at[c, d - 1], recv_sem=zr2_sem.at[c, d - 1],
            device_id=z_peer(d), device_id_type=MESH)

    def x_second(c, slot):
        d = turns[slot // 2][slot % 2]
        return pltpu.make_async_remote_copy(
            src_ref=xs2.at[c, slot], dst_ref=xr2.at[c, d - 1],
            send_sem=xs2_sem.at[c, d - 1], recv_sem=xr2_sem.at[c, d - 1],
            device_id=x_peer(d), device_id_type=MESH)

    def arrive(c, d, half):
        owner = lax.rem(me + 8 - d, 8)
        j = col_owner[owner]
        i = parts[half]
        lhs = jnp.concatenate([t5[2 * i * 8 + j], t5[(2 * i + 1) * 8 + j]], axis=0)
        if d == 0:
            nodes = send[c, 0, pl.ds(2 * i, 2)]
        else:
            nodes = recv[c, d - 1, pl.ds(2 * i, 2)]
        value = dot(lhs, nodes.reshape(2 * rank, width))
        for e in range(2):
            c5[2 * i + e, d] = keep(
                value[e * rank:(e + 1) * rank], ranks[0, 5, 0, (2 * i + e) * 8 + j])

    def quarters(c, half):
        pairs = tuple((k, dq, lax.rem(bx + dq, SIDE)) for k, dq in enumerate(turns[half]))
        for k, dq, q in pairs:
            for j in range(4):
                lhs = jnp.concatenate([t6[2 * q * 4 + j], t6[(2 * q + 1) * 4 + j]], axis=0)
                value = mix(lhs, c5[q, places[2 * j]], c5[q, places[2 * j + 1]])
                for e in range(2):
                    c6[k, e * 4 + j] = keep(
                        value[e * rank:(e + 1) * rank], ranks[0, 6, 0, (2 * q + e) * 4 + j])
        for k, dq, q in pairs:
            for i in range(2):
                for j in range(2):
                    base = (2 * q + i) * 4 + j
                    lhs = jnp.concatenate([t7[base], t7[base + 2]], axis=0)
                    value = mix(lhs, c6[k, i * 4 + 2 * j], c6[k, i * 4 + 2 * j + 1])
                    for e in range(2):
                        c7[k, (i * 2 + e) * 2 + j] = keep(
                            value[e * rank:(e + 1) * rank], ranks[0, 7, 0, base + 2 * e])
        for k, dq, q in pairs:
            for i in range(4):
                node = 4 * q + i
                value = mix(pair(t8, node), c7[k, 2 * i], c7[k, 2 * i + 1])
                for e in range(2):
                    c8[k, 2 * i + e] = keep(
                        value[e * rank:(e + 1) * rank], ranks[0, 8, 0, 2 * node + e])
        for k, dq, q in pairs:
            for m in range(4):
                xs[c, dq, m] = dot(row[8 * q + 2 * m], c8[k, 2 * m]).astype(jnp.bfloat16)
        for k, dq, q in pairs:
            for r in range(SIDE):
                m = lax.rem(bz + r, SIDE)
                zs[c, r, 2 * half + k] = dot(
                    row[8 * q + 2 * m + 1], c8[k, 2 * m + 1]).astype(jnp.bfloat16)
                if r == 0 and (half == 0 or k == 0):
                    x_first(c, dq).start()
        for d in (2, 1, 3):
            z_first(c, d, half).start()

    def phase_b(c):
        @pl.when(c == 0)
        def _():
            for i in range(5, 10):
                weight_in(i).wait()

        for half in range(2):
            arrive(c, 0, half)
            for k, d in enumerate(ARRIVALS):
                a2a(c, d, half).wait_recv()
                follow(c, half + (k + AHEAD) // 7, ARRIVALS[(k + AHEAD) % 7])
                arrive(c, d, half)
            quarters(c, half)
            if half == 0:
                @pl.when(c == chunks - 1)
                def _():
                    first_sum(c - 1)

    def wide(value):
        return value.astype(jnp.float32)

    def x_total(c, m):
        total = wide(xs[c, 0, m])
        for d in range(SIDE - 1):
            total = total + wide(xr[c, d, m])
        return total.astype(jnp.bfloat16)

    def z_total(c, slot):
        total = wide(zs[c, 0, slot])
        for d in range(SIDE - 1):
            total = total + wide(zr[c, d, slot])
        return total.astype(jnp.bfloat16)

    def first_sum(c):
        for d in (2, 1, 3):
            z_first(c, d, 0).wait_recv()
        for slot in range(2):
            xs2[c, slot] = z_total(c, slot)
        for d in (2, 1, 3):
            x_first(c, d).wait_recv()
        ready = None
        for r in (2, 1, 3):
            zs2[c, r] = x_total(c, lax.rem(bz + r, SIDE))
            if ready is None:
                for slot in range(2):
                    x_second(c, slot).start()
            else:
                z_second(c, ready).start()
            ready = r
        for d in (2, 1, 3):
            z_first(c, d, 1).wait_recv()
        xs2[c, 2] = z_total(c, 2)
        z_second(c, ready).start()
        zs2[c, 0] = x_total(c, bz)
        x_second(c, 2).start()
        xs2[c, 3] = z_total(c, 3)

    def last_sum(c):
        columns = pl.ds(pl.multiple_of(c * width, width), width)
        for d in (1, 3, 2):
            z_second(c, d).wait_recv()
        total = wide(zs2[c, 0])
        for d in range(SIDE - 1):
            total = total + wide(zr2[c, d])
        out[pl.ds(0, rank), columns] = total.astype(jnp.bfloat16)
        for slot in range(SIDE - 1):
            x_second(c, slot).wait_recv()
        total = wide(xs2[c, SIDE - 1])
        for d in range(SIDE - 1):
            total = total + wide(xr2[c, d])
        out[pl.ds(rank, rank), columns] = total.astype(jnp.bfloat16)

    weight_in(1).start()

    def drain(c):
        for d in range(1, 8):
            for half in range(2):
                a2a(c, d, half).wait_send()
        for d in range(1, SIDE):
            x_first(c, d).wait_send()
            for half in range(2):
                z_first(c, d, half).wait_send()
            x_second(c, d - 1).wait_send()
            z_second(c, d).wait_send()

    phase_a(False)
    phase_a(True)

    @pl.loop(0, chunks)
    def _(c):
        phase_b(c)

        @pl.when((c >= 1) & (c < chunks - 1))
        def _():
            first_sum(c - 1)

        @pl.when(c >= 2)
        def _():
            last_sum(c - 2)

    first_sum(chunks - 1)
    last_sum(chunks - 2)

    @pl.loop(0, chunks - 1)
    def _(c):
        drain(c)

    last_sum(chunks - 1)

    drain(chunks - 1)


def local(columns_in, leaf_basis, transfers, row_basis, ranks, col_owner, row_owner):
    nodes, leaf_size, rank = leaf_basis.shape[2:]
    sides = columns_in.shape[3]
    levels = transfers.shape[1]
    width = 128
    chunks = sides // width
    rest = sides - width
    bf = jnp.bfloat16
    dma = pltpu.SemaphoreType.DMA
    hbm = pl.BlockSpec(memory_space=pltpu.HBM)
    smem = pl.BlockSpec(memory_space=pltpu.SMEM)
    tile = (rank, width)
    scratch = [pltpu.VMEM((nodes, leaf_size, width), bf), pltpu.VMEM((nodes, leaf_size, rest), bf)]
    scratch += [pltpu.VMEM((nodes, leaf_size, rank), bf)]
    scratch += [pltpu.VMEM((nodes, rank, 2 * rank), bf)] * levels
    scratch += [pltpu.VMEM((nodes, leaf_size, rank), bf)]
    scratch += [pltpu.VMEM((nodes, rank, width), bf)] * 2 + [pltpu.VMEM((nodes, rank, rest), bf)] * 2
    scratch += [pltpu.VMEM((chunks, 8, 4) + tile, bf), pltpu.VMEM((chunks, 7, 4) + tile, bf)]
    scratch += [pltpu.VMEM((4, 8) + tile, bf)] + [pltpu.VMEM((2, 8) + tile, bf)] * 3
    scratch += [pltpu.VMEM((chunks, 4, 4) + tile, bf)] * 2
    scratch += [pltpu.VMEM((chunks, 3, 4) + tile, bf)] * 2
    scratch += [pltpu.VMEM((chunks, 4) + tile, bf)] * 2
    scratch += [pltpu.VMEM((chunks, 3) + tile, bf)] * 2
    scratch += [dma((10,)), dma((2,)), dma((chunks, 7, 2)), dma((chunks, 7, 2))]
    scratch += [dma((chunks, 3))] * 2 + [dma((chunks, 3, 2))] * 2 + [dma((chunks, 3))] * 4
    share = nodes * leaf_size // lax.axis_size("blk")
    result = pl.pallas_call(
        functools.partial(kernel, chunks, width, rank),
        out_shape=jax.ShapeDtypeStruct((share, sides), bf),
        in_specs=[hbm] * 4 + [smem] * 3,
        out_specs=pl.BlockSpec(memory_space=pltpu.VMEM),
        scratch_shapes=scratch,
        compiler_params=pltpu.CompilerParams(
            collective_id=0, has_side_effects=True, vmem_limit_bytes=60 * 1024 * 1024),
        name="block_row",
    )(
        columns_in.reshape(nodes, leaf_size, sides),
        leaf_basis[0, 0],
        transfers[0, :, 0],
        row_basis[0, 0],
        ranks,
        col_owner,
        row_owner,
    )
    return result.reshape(1, share, sides)


def solution(mesh):
    return jax.shard_map(
        local,
        mesh=mesh,
        in_specs=(
            P("blk", "leaf", None, None),
            P("blk", "leaf", None, None, None),
            P("blk", None, "leaf", None, None, None),
            P("blk", "leaf", None, None, None),
            P("blk", None, "leaf", None),
            P(),
            P(),
        ),
        out_specs=P("leaf", "blk", None),
        check_vma=False,
    )
```
